32 devices in a mesh: seq: 8 (over z, x), chan: 4 (over y, core).
Axes of the slice: x: 2, y: 2, z: 4, core: 2. Of those that a mesh axis runs over, the one named last changes fastest.
Arguments:
- values: bfloat16 [2048, 4096], P('seq', 'chan'), may hold values from -6 to 6
- gates: bfloat16 [2048, 4096], P('seq', 'chan'), may hold values from -6 to 6
- filters: float32 [2048, 4096], P('seq', 'chan'), may hold values from -4 to 4
- skip: float32 [4096], P('chan'), may hold values from -1 to 1
- w_out: bfloat16 [4096, 4096], P(None, 'chan'), may hold values from -0.09375 to 0.09375
Outputs:
- output: bfloat16 [2048, 4096], P('seq', 'chan')
The draws below stay inside these ranges and needn't reach their ends.
All inputs are finite; a program needn't handle non-finite values.
Results may differ from the reference program's by a relative error of at most 0.0056.
Values may be sent and summed in bfloat16 or wider, within the bound.
A program may use at most 128 MiB of HBM per device.

```python
import jax
import jax.numpy as jnp
from jax import lax

D = 4096
TOKENS = 2048


def draw_filters(key, part):
    rate_key, noise_key = jax.random.split(key)
    lags = lax.iota(jnp.float32, TOKENS)[:, None]
    log_rate = jax.random.uniform(rate_key, (1, D), jnp.float32, jnp.log(0.01 / TOKENS), jnp.log(1.0 / 30.0))
    noise = jax.random.truncated_normal(noise_key, -4.0, 4.0, (TOKENS, D), jnp.float32)
    rate = jnp.exp(log_rate)
    scale = jnp.sqrt(1.0 - jnp.exp(-2.0 * rate))
    return noise * scale * jnp.exp(-rate * lags)


def level_of(stream_key, dims, cuts, least, high):
    def one(position, blocks):
        heights = jax.random.uniform(jax.random.fold_in(jax.random.fold_in(stream_key, 6), position), (blocks,), jnp.float32, least / len(cuts), high / len(cuts))
        return jnp.repeat(jnp.exp(heights), dims[position] // blocks).reshape((-1,) + (1,) * (len(dims) - position - 1))

    gain = one(*cuts[0])
    for cut in cuts[1:]:
        gain = gain * one(*cut)
    return gain


def scatter_about(stream_key, extent, deviation, reach, cuts=(), held_as=jnp.bfloat16):
    entries = deviation * jax.random.normal(stream_key, extent, jnp.float32)
    if cuts:
        entries = entries * level_of(stream_key, extent, cuts, -0.22, 0.18)
    return jnp.clip(entries, -reach, reach).astype(held_as)


def setup_inputs(seed: int = 0) -> dict:
    keys = jax.random.split(jax.random.key(seed), 6)
    return {
        "values": scatter_about(keys[0], (TOKENS, D), 1.0, 6.0, ((0, 8), (1, 4))),
        "gates": scatter_about(keys[1], (TOKENS, D), 1.0, 6.0, ((0, 8), (1, 4))),
        "filters": draw_filters(jax.random.fold_in(keys[5], 71), 0),
        "skip": jnp.clip(jax.random.uniform(keys[3], (D,), jnp.float32, -1.0, 1.0) * level_of(keys[3], (D,), ((0, 4),), -0.4, 0.0), -1.0, 1.0),
        "w_out": scatter_about(keys[4], (D, D), D ** -0.5, 0.09375, ((1, 4),)),
    }


def reference(values, gates, filters, skip, w_out):
    length = values.shape[0]
    channels = values.shape[1]
    block_width = min(512, channels)
    block_count = channels // block_width
    signal = values.astype(jnp.float32).T.reshape(block_count, block_width, length)
    kernel = filters.astype(jnp.float32).T.reshape(block_count, block_width, length)

    def convolve(operands):
        signal_block, kernel_block = operands
        spectrum = jnp.fft.rfft(signal_block, n=2 * length, axis=1) * jnp.fft.rfft(kernel_block, n=2 * length, axis=1)
        return jnp.fft.irfft(spectrum, n=2 * length, axis=1)[:, :length]

    causal = lax.map(convolve, (signal, kernel)).reshape(channels, length).T.astype(jnp.bfloat16)
    mixed = (gates.astype(jnp.float32) * (causal.astype(jnp.float32) + skip[None, :] * values.astype(jnp.float32))).astype(jnp.bfloat16)
    return jnp.dot(mixed, w_out, preferred_element_type=jnp.float32).astype(jnp.bfloat16)
```

```python
import functools
import math

import jax
import jax.numpy as jnp
import numpy as np
from jax import lax
from jax.experimental import pallas as pl
from jax.experimental.pallas import tpu as pltpu
from jax.sharding import PartitionSpec as P

LANES = 128
STRIP = 16
MESH = pl.DeviceIdType.MESH


def product(form, left, right):
    return jnp.einsum(
        form, left, right, precision=lax.Precision.HIGHEST, preferred_element_type=jnp.float32
    )


def phase(first_count, second_count, modulus):
    left = lax.iota(jnp.int32, first_count)[:, None]
    right = lax.iota(jnp.int32, second_count)[None, :]
    angle = (left * right % modulus).astype(jnp.float32) * (2.0 * math.pi / modulus)
    return (jnp.cos(angle), jnp.sin(angle))


def spectral_conv(chan_values, chan_filter):
    nchan = chan_values.shape[0]
    length = chan_values.shape[1]
    summed = 2 * length
    columns = 128
    row_count = summed // columns
    half_rows = row_count // 2
    cos_rows, sin_rows = phase(row_count, half_rows, row_count)
    cos_twist, sin_twist = phase(row_count, columns, summed)
    cos_cols, sin_cols = phase(columns, columns, columns)
    cos_back, sin_back = phase(half_rows, row_count, row_count)

    def forward(signal):
        grid = signal.astype(jnp.float32).reshape(nchan, half_rows, columns)
        real_a = product("kn,cna->cka", cos_rows, grid)
        imag_a = -product("kn,cna->cka", sin_rows, grid)
        real_b = real_a * cos_twist + imag_a * sin_twist
        imag_b = imag_a * cos_twist - real_a * sin_twist
        real_c = product("cka,am->ckm", real_b, cos_cols) + product("cka,am->ckm", imag_b, sin_cols)
        imag_c = product("cka,am->ckm", imag_b, cos_cols) - product("cka,am->ckm", real_b, sin_cols)
        return (real_c, imag_c)

    real_v, imag_v = forward(chan_values)
    real_h, imag_h = forward(chan_filter)
    real_p = real_v * real_h - imag_v * imag_h
    imag_p = real_v * imag_h + imag_v * real_h
    real_d = product("ckm,ma->cka", real_p, cos_cols) - product("ckm,ma->cka", imag_p, sin_cols)
    imag_d = product("ckm,ma->cka", imag_p, cos_cols) + product("ckm,ma->cka", real_p, sin_cols)
    real_e = real_d * cos_twist - imag_d * sin_twist
    imag_e = imag_d * cos_twist + real_d * sin_twist
    result = product("nk,cka->cna", cos_back, real_e) - product("nk,cka->cna", sin_back, imag_e)
    return (result * (1.0 / summed)).reshape(nchan, length).astype(jnp.bfloat16)


def per_device_generic(values, gates, filters, skip, w_out):
    value_trans = values.T
    filter_trans = filters.T
    chan_values = lax.all_to_all(value_trans, "seq", split_axis=0, concat_axis=1, tiled=True)
    chan_filter = lax.all_to_all(filter_trans, "seq", split_axis=0, concat_axis=1, tiled=True)
    convolved = spectral_conv(chan_values, chan_filter)
    causal_trans = lax.all_to_all(convolved, "seq", split_axis=1, concat_axis=0, tiled=True)
    causal = causal_trans.T
    mixed = (
        gates.astype(jnp.float32)
        * (causal.astype(jnp.float32) + skip[None, :] * values.astype(jnp.float32))
    ).astype(jnp.bfloat16)
    projected = jnp.dot(
        lax.all_gather(mixed, "chan", axis=1, tiled=True), w_out, preferred_element_type=jnp.float32
    )
    return projected.astype(jnp.bfloat16)


def split(x):
    high = x.astype(jnp.bfloat16)
    return high, (x - high.astype(jnp.float32)).astype(jnp.bfloat16)


def tables(block):
    index = np.arange(block)
    angle = np.pi * (np.outer(4 * index + 1, index) % (4 * block)) / (2 * block)
    whole = np.concatenate([np.cos(angle), -np.sin(angle)]).astype(np.float32)
    high = whole.astype(jnp.bfloat16)
    both = np.stack([high, (whole - high.astype(np.float32)).astype(jnp.bfloat16)])
    back = (both.astype(np.float32) / block).astype(jnp.bfloat16)
    return both, np.ascontiguousarray(back.transpose(0, 2, 1))


def kernel(
    blocks, chans, chunks,
    values_hbm, gates_hbm, filters_hbm, skip, forward_hbm, backward_hbm, w_hbm,
    out,
    values, gates, filters, h_send, got, forward, backward, spec, y, y_send, causal, mixed, w, acc,
    l_sem, sent, gate, in_sem, n_sem, x_sem, an_sem, ax_sem, bn_sem, bx_sem, fn_sem, fx_sem,
):
    me = lax.axis_index("seq")
    mine = lax.axis_index("chan")
    block = values.shape[0]
    depth = values.shape[1]
    half = blocks // 2
    left, right = pl.ds(0, LANES), pl.ds(LANES, LANES)
    every = pl.ds(0, block)
    near = list(range(1, half))
    upper = me // half
    seat = lax.rem(me, half)
    other = half - half * upper
    odd = lax.rem(me, 2)

    def lanes(position):
        return pl.ds(pl.multiple_of(position * LANES, LANES), LANES)

    def partner(mask):
        place = me
        bit = 1
        while bit < half:
            if mask & bit:
                place = place + bit - 2 * bit * lax.rem(place // bit, 2)
            bit *= 2
        return place

    places = [partner(mask) for mask in range(half)]

    local = [
        pltpu.make_async_copy(source, target, l_sem.at[i])
        for i, (source, target) in enumerate((
            (filters_hbm, filters), (values_hbm, values), (values_hbm.at[:, lanes(me)], got.at[me, :, left]),
            (forward_hbm, forward), (backward_hbm, backward), (gates_hbm, gates), (w_hbm, w),
        ))
    ]
    filters_copy, values_copy, own_copy, forward_copy, backward_copy, gates_copy, w_copy = local
    for copy in local:
        copy.start()

    sibling = mine + 1 - 2 * lax.rem(mine, 2)
    across = lax.rem(mine + 2, chans)
    opposite = lax.rem(sibling + 2, chans)
    barrier = pltpu.get_barrier_semaphore()
    for place in places[1:] + [other + t for t in range(half)]:
        pl.semaphore_signal(barrier, inc=1, device_id={"seq": place}, device_id_type=MESH)
    for chan in (sibling, across):
        pl.semaphore_signal(barrier, inc=1, device_id={"chan": chan}, device_id_type=MESH)
    filters_copy.wait()
    h_send[...] = filters[...].astype(jnp.bfloat16)
    pl.semaphore_wait(barrier, blocks + 1)

    def remote(source, target, sem, where, out_sem=None):
        return pltpu.make_async_remote_copy(
            src_ref=source, dst_ref=target, send_sem=sent.at[0] if out_sem is None else out_sem, recv_sem=sem,
            device_id=where, device_id_type=MESH,
        )

    def across_cut(phase):
        return [other + 2 * phase + odd, other + 2 * phase + 1 - odd]

    def send_in(place):
        remote(values_hbm.at[:, lanes(place)], got.at[me, :, left], in_sem.at[me], {"seq": place}).start()
        remote(h_send.at[:, lanes(place)], got.at[me, :, right], in_sem.at[me], {"seq": place}).start()

    for place in across_cut(0) + across_cut(1) + places[1:]:
        send_in(place)
    got[me, :, LANES:] = h_send[:, lanes(me)]
    own_copy.wait()
    forward_copy.wait()

    def transform(place):
        x = got[place]
        spec[place] = jnp.dot(forward[0], x, preferred_element_type=jnp.float32) + jnp.dot(
            forward[1], x, preferred_element_type=jnp.float32
        )

    def take_in(place):
        spot = got.at[place]
        remote(spot, spot, in_sem.at[place], {"seq": other}).wait_recv()
        transform(place)

    def combine(pair):
        def body(strip, _):
            parts = []
            for part in range(STRIP // 8):
                re_rows = pl.ds(pl.multiple_of(strip * STRIP + 8 * part, 8), 8)
                im_rows = pl.ds(pl.multiple_of(block + strip * STRIP + 8 * part, 8), 8)
                count = pair[-1] + 1
                v = [(spec[n, re_rows, :LANES], spec[n, im_rows, :LANES]) for n in range(count)]
                h = [(spec[n, re_rows, LANES:], spec[n, im_rows, LANES:]) for n in range(count)]
                g = [h[0]] + [(h[n][0] - h[n - 1][1], h[n][1] + h[n - 1][0]) for n in range(1, count)]
                sums = []
                for k in pair:
                    re = im = None
                    for n in range(k + 1):
                        (a, b), (c, d) = v[n], g[k - n]
                        re_term, im_term = a * c - b * d, a * d + b * c
                        re = re_term if re is None else re + re_term
                        im = im_term if im is None else im + im_term
                    sums.append((re, im))
                parts.append(sums)
            for i in (0, 1):
                for which in (0, 1):
                    high, low = split(jnp.concatenate([sums[i][which] for sums in parts], axis=0))
                    rows = pl.ds(pl.multiple_of(which * block + strip * STRIP, STRIP), STRIP)
                    y[0, pair[0] // 2, rows, i * LANES : (i + 1) * LANES] = high
                    y[1, pair[0] // 2, rows, i * LANES : (i + 1) * LANES] = low
            return 0

        lax.fori_loop(0, block // STRIP, body, 0)

    def produce(rank):
        pair = (2 * rank, 2 * rank + 1)
        combine(pair)
        high, low = y[0, rank], y[1, rank]
        x = (
            jnp.dot(backward[0], high, preferred_element_type=jnp.float32)
            + jnp.dot(backward[1], high, preferred_element_type=jnp.float32)
            + jnp.dot(backward[0], low, preferred_element_type=jnp.float32)
        ).astype(jnp.bfloat16)
        y_send[pair[0]] = x[:, :LANES]
        y_send[pair[1]] = x[:, LANES:]

    def send_near():
        for mask in near:
            remote(y_send.at[places[mask]], causal.at[mask], n_sem.at[mask], {"seq": places[mask]}).start()

    def send_cross(phase, q):
        start, size = chunks[q]
        rows = pl.ds(start, size)
        for place in across_cut(phase):
            remote(
                y_send.at[place, rows], causal.at[half + seat, rows], x_sem.at[q], {"seq": place},
                gate.at[phase * len(chunks) + q],
            ).start()

    def gone(phase, q):
        spot = causal.at[0]
        remote(spot, spot, x_sem.at[q], {"seq": other}, gate.at[phase * len(chunks) + q]).wait_send()

    def slot(chan, mask):
        return mixed.at[chan, mask // 2, :, lanes(lax.rem(places[mask], 2))]

    def far_slot(chan, q):
        start, size = chunks[q]
        return mixed.at[chan, pl.ds(half // 2, half // 2), pl.ds(start, size)]

    def blend(place, y_rows, rows, target):
        cols = lanes(place)
        direct = skip[:, cols] * values[rows, cols].astype(jnp.float32)
        target[rows, :] = (gates[rows, cols].astype(jnp.float32) * (y_rows.astype(jnp.float32) + direct)).astype(
            jnp.bfloat16
        )

    def share(spot, a_sem, b_sem):
        remote(spot, spot, a_sem, {"chan": across}).start()
        remote(spot, spot, b_sem, {"chan": sibling}).start()

    def near_in(mask):
        if mask:
            spot = causal.at[mask]
            remote(spot, spot, n_sem.at[mask], {"seq": places[mask]}).wait_recv()
            blend(places[mask], causal[mask], every, slot(mine, mask))
        else:
            blend(me, y_send[me], every, slot(mine, mask))
        share(slot(mine, mask), an_sem.at[mask], bn_sem.at[mask])

    def cross_in(q):
        start, size = chunks[q]
        rows = pl.ds(start, size)
        spot = causal.at[pl.ds(half, half), rows]
        remote(spot, spot, x_sem.at[q], {"seq": other}).wait_recv()
        for t in range(half):
            blend(other + t, causal[half + t, rows], rows, mixed.at[mine, (half + t) // 2, :, lanes(t % 2)])
        share(far_slot(mine, q), ax_sem.at[q], bx_sem.at[q])

    def near_on(mask):
        spot = slot(across, mask)
        remote(spot, spot, an_sem.at[mask], {"chan": across}).wait_recv()
        remote(spot, spot, fn_sem.at[mask], {"chan": sibling}).start()

    def cross_on(q):
        spot = far_slot(across, q)
        remote(spot, spot, ax_sem.at[q], {"chan": across}).wait_recv()
        remote(spot, spot, fx_sem.at[q], {"chan": sibling}).start()

    def arrived(spot, sem):
        remote(spot, spot, sem, {"chan": sibling}).wait_recv()

    def project(ranks, start, size, pair, first, last):
        rows = pl.ds(start, size)

        def tile(n, _):
            cols = pl.ds(pl.multiple_of(n * 512, 512), 512)
            total = None
            for chan in pair:
                for rank in ranks:
                    source = places[2 * rank] // 2 if 2 * rank < half else other // 2 + rank - half // 2
                    deep = pl.ds(pl.multiple_of(chan * depth + source * 2 * LANES, 2 * LANES), 2 * LANES)
                    term = jnp.dot(mixed[chan, rank, rows], w[deep, cols], preferred_element_type=jnp.float32)
                    total = term if total is None else total + term
            if not first:
                total = total + acc[rows, cols]
            if last:
                out[rows, cols] = total.astype(out.dtype)
            else:
                acc[rows, cols] = total
            return 0

        lax.fori_loop(0, out.shape[1] // 512, tile, 0)

    close, far = range(half // 2), range(half // 2, half)
    masks = [0] + near

    def near_first():
        for mask in masks:
            arrived(slot(sibling, mask), bn_sem.at[mask])
        project(close, 0, block, (mine, sibling), True, False)

    def near_second():
        for mask in masks:
            arrived(slot(opposite, mask), fn_sem.at[mask])
        project(close, 0, block, (across, opposite), False, False)

    def cross_first(q):
        arrived(far_slot(sibling, q), bx_sem.at[q])
        project(far, *chunks[q], (mine, sibling), False, False)

    def cross_second(q):
        arrived(far_slot(opposite, q), fx_sem.at[q])
        project(far, *chunks[q], (across, opposite), False, True)

    transform(me)
    for mask in near:
        take_in(places[mask])
    backward_copy.wait()
    values_copy.wait()
    gates_copy.wait()

    @pl.when(upper == 0)
    def _():
        for rank in range(half // 2):
            produce(rank)
        send_near()
        near_in(0)
        for phase in range(half // 2):
            rank = half // 2 + phase
            take_in(2 * rank)
            take_in(2 * rank + 1)
            produce(rank)
            if phase == 0:
                send_cross(0, 0)
                send_cross(0, 1)

    @pl.when(upper == 1)
    def _():
        for rank in range(half // 2):
            take_in(2 * rank)
            take_in(2 * rank + 1)
            if rank == 0:
                produce(rank)
                send_cross(0, 0)
                send_cross(0, 1)
        for rank in range(half // 2, half):
            produce(rank)
        send_near()
        for rank in range(1, half // 2):
            produce(rank)
        near_in(0)

    w_copy.wait()
    gone(0, 0)
    gone(0, 1)
    send_cross(1, 0)
    send_cross(1, 1)
    for mask in near:
        near_in(mask)
    near_on(0)
    cross_in(0)
    for mask in near:
        near_on(mask)
    near_first()
    cross_in(1)
    cross_on(0)
    near_second()
    cross_first(0)
    cross_on(1)
    cross_second(0)
    cross_first(1)
    cross_second(1)
    gone(1, 0)
    gone(1, 1)
    whole = w.at[pl.ds(0, (3 * (blocks - 1) + 3 * blocks - half) * block * LANES // w.shape[1])]
    remote(whole, whole, in_sem.at[0], {"chan": sibling}).wait_send()


def per_device_fused(blocks, chans, values, gates, filters, skip, w_out):
    block, width = values.shape
    forward, backward = tables(block)
    vmem = pl.BlockSpec(memory_space=pltpu.VMEM)
    hbm = pl.BlockSpec(memory_space=pl.ANY)
    out_width = w_out.shape[1]
    chunks = [(q * block // 2, block // 2) for q in range(2)]

    def sems(*shape):
        return pltpu.SemaphoreType.DMA(shape)

    half, pieces = blocks // 2, len(chunks)
    return pl.pallas_call(
        functools.partial(kernel, blocks, chans, chunks),
        out_shape=jax.ShapeDtypeStruct((block, out_width), jnp.bfloat16),
        in_specs=[hbm, hbm, hbm, vmem, hbm, hbm, hbm],
        out_specs=vmem,
        scratch_shapes=[
            pltpu.VMEM((block, width), jnp.bfloat16),
            pltpu.VMEM((block, width), jnp.bfloat16),
            pltpu.VMEM((block, width), jnp.float32),
            pltpu.VMEM((block, width), jnp.bfloat16),
            pltpu.VMEM((blocks, block, 2 * LANES), jnp.bfloat16),
            pltpu.VMEM(forward.shape, jnp.bfloat16),
            pltpu.VMEM(backward.shape, jnp.bfloat16),
            pltpu.VMEM((blocks, 2 * block, 2 * LANES), jnp.float32),
            pltpu.VMEM((2, half, 2 * block, 2 * LANES), jnp.bfloat16),
            pltpu.VMEM((blocks, block, LANES), jnp.bfloat16),
            pltpu.VMEM((blocks, block, LANES), jnp.bfloat16),
            pltpu.VMEM((chans, half, block, 2 * LANES), jnp.bfloat16),
            pltpu.VMEM(w_out.shape, jnp.bfloat16),
            pltpu.VMEM((block, out_width), jnp.float32),
            sems(7), sems(1), sems(half), sems(blocks), sems(half), sems(pieces),
        ]
        + [sems(half), sems(pieces)] * 3,
        compiler_params=pltpu.CompilerParams(
            collective_id=0, has_side_effects=True, vmem_limit_bytes=56 * 2**20
        ),
    )(values, gates, filters, skip[None, :], jnp.asarray(forward), jnp.asarray(backward), w_out)


def per_device(mesh_shape, values, gates, filters, skip, w_out):
    blocks, chans = mesh_shape["seq"], mesh_shape["chan"]
    block, width = values.shape
    fits = (
        width == blocks * LANES and chans == 4 and blocks == 8 and block == 256
        and w_out.shape[0] == chans * width and w_out.shape[1] == 1024
    )
    if fits:
        return per_device_fused(blocks, chans, values, gates, filters, skip, w_out)
    return per_device_generic(values, gates, filters, skip, w_out)


def solution(mesh):
    placed = (P("seq", "chan"), P("seq", "chan"), P("seq", "chan"), P("chan"), P(None, "chan"))
    return jax.shard_map(
        functools.partial(per_device, dict(mesh.shape)),
        mesh=mesh, in_specs=placed, out_specs=P("seq", "chan"), check_vma=False,
    )
```

```python
import functools
import math

import jax
import jax.numpy as jnp
import numpy as np
from jax import lax
from jax.experimental import pallas as pl
from jax.experimental.pallas import tpu as pltpu
from jax.sharding import PartitionSpec as P

LANES = 128
STRIP = 16
MESH = pl.DeviceIdType.MESH


def product(form, left, right):
    return jnp.einsum(
        form, left, right, precision=lax.Precision.HIGHEST, preferred_element_type=jnp.float32
    )


def phase(first_count, second_count, modulus):
    left = lax.iota(jnp.int32, first_count)[:, None]
    right = lax.iota(jnp.int32, second_count)[None, :]
    angle = (left * right % modulus).astype(jnp.float32) * (2.0 * math.pi / modulus)
    return (jnp.cos(angle), jnp.sin(angle))


def spectral_conv(chan_values, chan_filter):
    nchan = chan_values.shape[0]
    length = chan_values.shape[1]
    summed = 2 * length
    columns = 128
    row_count = summed // columns
    half_rows = row_count // 2
    cos_rows, sin_rows = phase(row_count, half_rows, row_count)
    cos_twist, sin_twist = phase(row_count, columns, summed)
    cos_cols, sin_cols = phase(columns, columns, columns)
    cos_back, sin_back = phase(half_rows, row_count, row_count)

    def forward(signal):
        grid = signal.astype(jnp.float32).reshape(nchan, half_rows, columns)
        real_a = product("kn,cna->cka", cos_rows, grid)
        imag_a = -product("kn,cna->cka", sin_rows, grid)
        real_b = real_a * cos_twist + imag_a * sin_twist
        imag_b = imag_a * cos_twist - real_a * sin_twist
        real_c = product("cka,am->ckm", real_b, cos_cols) + product("cka,am->ckm", imag_b, sin_cols)
        imag_c = product("cka,am->ckm", imag_b, cos_cols) - product("cka,am->ckm", real_b, sin_cols)
        return (real_c, imag_c)

    real_v, imag_v = forward(chan_values)
    real_h, imag_h = forward(chan_filter)
    real_p = real_v * real_h - imag_v * imag_h
    imag_p = real_v * imag_h + imag_v * real_h
    real_d = product("ckm,ma->cka", real_p, cos_cols) - product("ckm,ma->cka", imag_p, sin_cols)
    imag_d = product("ckm,ma->cka", imag_p, cos_cols) + product("ckm,ma->cka", real_p, sin_cols)
    real_e = real_d * cos_twist - imag_d * sin_twist
    imag_e = imag_d * cos_twist + real_d * sin_twist
    result = product("nk,cka->cna", cos_back, real_e) - product("nk,cka->cna", sin_back, imag_e)
    return (result * (1.0 / summed)).reshape(nchan, length).astype(jnp.bfloat16)


def per_device_generic(values, gates, filters, skip, w_out):
    value_trans = values.T
    filter_trans = filters.T
    chan_values = lax.all_to_all(value_trans, "seq", split_axis=0, concat_axis=1, tiled=True)
    chan_filter = lax.all_to_all(filter_trans, "seq", split_axis=0, concat_axis=1, tiled=True)
    convolved = spectral_conv(chan_values, chan_filter)
    causal_trans = lax.all_to_all(convolved, "seq", split_axis=1, concat_axis=0, tiled=True)
    causal = causal_trans.T
    mixed = (
        gates.astype(jnp.float32)
        * (causal.astype(jnp.float32) + skip[None, :] * values.astype(jnp.float32))
    ).astype(jnp.bfloat16)
    projected = jnp.dot(
        lax.all_gather(mixed, "chan", axis=1, tiled=True), w_out, preferred_element_type=jnp.float32
    )
    return projected.astype(jnp.bfloat16)


def split(x):
    high = x.astype(jnp.bfloat16)
    return high, (x - high.astype(jnp.float32)).astype(jnp.bfloat16)


def tables(block):
    index = np.arange(block)
    angle = np.pi * (np.outer(4 * index + 1, index) % (4 * block)) / (2 * block)
    whole = np.concatenate([np.cos(angle), -np.sin(angle)]).astype(np.float32)
    high = whole.astype(jnp.bfloat16)
    both = np.stack([high, (whole - high.astype(np.float32)).astype(jnp.bfloat16)])
    back = (both.astype(np.float32) / block).astype(jnp.bfloat16)
    return both, np.ascontiguousarray(back.transpose(0, 2, 1))


def kernel(
    blocks, chans, chunks,
    values_hbm, gates_hbm, filters_hbm, skip, forward_hbm, backward_hbm, w_hbm,
    out,
    values, gates, filters, h_send, got, forward, backward, spec, y, y_send, causal, mixed, w, acc,
    l_sem, sent, gate, in_sem, n_sem, x_sem, an_sem, ax_sem, bn_sem, bx_sem, fn_sem, fx_sem,
):
    me = lax.axis_index("seq")
    mine = lax.axis_index("chan")
    block = values.shape[0]
    depth = values.shape[1]
    half = blocks // 2
    left, right = pl.ds(0, LANES), pl.ds(LANES, LANES)
    every = pl.ds(0, block)
    near = list(range(1, half))
    upper = me // half
    seat = lax.rem(me, half)
    other = half - half * upper
    odd = lax.rem(me, 2)

    def lanes(position):
        return pl.ds(pl.multiple_of(position * LANES, LANES), LANES)

    def partner(mask):
        place = me
        bit = 1
        while bit < half:
            if mask & bit:
                place = place + bit - 2 * bit * lax.rem(place // bit, 2)
            bit *= 2
        return place

    places = [partner(mask) for mask in range(half)]

    local = [
        pltpu.make_async_copy(source, target, l_sem.at[i])
        for i, (source, target) in enumerate((
            (filters_hbm, filters), (values_hbm, values), (values_hbm.at[:, lanes(me)], got.at[me, :, left]),
            (forward_hbm, forward), (backward_hbm, backward), (gates_hbm, gates), (w_hbm, w),
        ))
    ]
    filters_copy, values_copy, own_copy, forward_copy, backward_copy, gates_copy, w_copy = local
    for copy in local:
        copy.start()

    sibling = mine + 1 - 2 * lax.rem(mine, 2)
    across = lax.rem(mine + 2, chans)
    opposite = lax.rem(sibling + 2, chans)
    barrier = pltpu.get_barrier_semaphore()
    for place in places[1:] + [other + t for t in range(half)]:
        pl.semaphore_signal(barrier, inc=1, device_id={"seq": place}, device_id_type=MESH)
    for chan in (sibling, across):
        pl.semaphore_signal(barrier, inc=1, device_id={"chan": chan}, device_id_type=MESH)
    filters_copy.wait()
    h_send[...] = filters[...].astype(jnp.bfloat16)
    pl.semaphore_wait(barrier, blocks + 1)

    def remote(source, target, sem, where, out_sem=None):
        return pltpu.make_async_remote_copy(
            src_ref=source, dst_ref=target, send_sem=sent.at[0] if out_sem is None else out_sem, recv_sem=sem,
            device_id=where, device_id_type=MESH,
        )

    def across_cut(phase):
        return [other + 2 * phase + odd, other + 2 * phase + 1 - odd]

    def send_in(place):
        remote(values_hbm.at[:, lanes(place)], got.at[me, :, left], in_sem.at[me], {"seq": place}).start()
        remote(h_send.at[:, lanes(place)], got.at[me, :, right], in_sem.at[me], {"seq": place}).start()

    for place in across_cut(0) + across_cut(1) + places[1:]:
        send_in(place)
    got[me, :, LANES:] = h_send[:, lanes(me)]
    own_copy.wait()
    forward_copy.wait()

    def transform(place):
        x = got[place]
        spec[place] = jnp.dot(forward[0], x, preferred_element_type=jnp.float32) + jnp.dot(
            forward[1], x, preferred_element_type=jnp.float32
        )

    def take_in(place):
        spot = got.at[place]
        remote(spot, spot, in_sem.at[place], {"seq": other}).wait_recv()
        transform(place)

    def combine(pair):
        def body(strip, _):
            parts = []
            for part in range(STRIP // 8):
                re_rows = pl.ds(pl.multiple_of(strip * STRIP + 8 * part, 8), 8)
                im_rows = pl.ds(pl.multiple_of(block + strip * STRIP + 8 * part, 8), 8)
                count = pair[-1] + 1
                v = [(spec[n, re_rows, :LANES], spec[n, im_rows, :LANES]) for n in range(count)]
                h = [(spec[n, re_rows, LANES:], spec[n, im_rows, LANES:]) for n in range(count)]
                g = [h[0]] + [(h[n][0] - h[n - 1][1], h[n][1] + h[n - 1][0]) for n in range(1, count)]
                sums = []
                for k in pair:
                    re = im = None
                    for n in range(k + 1):
                        (a, b), (c, d) = v[n], g[k - n]
                        re_term, im_term = a * c - b * d, a * d + b * c
                        re = re_term if re is None else re + re_term
                        im = im_term if im is None else im + im_term
                    sums.append((re, im))
                parts.append(sums)
            for i in (0, 1):
                for which in (0, 1):
                    high, low = split(jnp.concatenate([sums[i][which] for sums in parts], axis=0))
                    rows = pl.ds(pl.multiple_of(which * block + strip * STRIP, STRIP), STRIP)
                    y[0, pair[0] // 2, rows, i * LANES : (i + 1) * LANES] = high
                    y[1, pair[0] // 2, rows, i * LANES : (i + 1) * LANES] = low
            return 0

        lax.fori_loop(0, block // STRIP, body, 0)

    def produce(rank):
        pair = (2 * rank, 2 * rank + 1)
        combine(pair)
        high, low = y[0, rank], y[1, rank]
        x = (
            jnp.dot(backward[0], high, preferred_element_type=jnp.float32)
            + jnp.dot(backward[1], high, preferred_element_type=jnp.float32)
            + jnp.dot(backward[0], low, preferred_element_type=jnp.float32)
        ).astype(jnp.bfloat16)
        y_send[pair[0]] = x[:, :LANES]
        y_send[pair[1]] = x[:, LANES:]

    def send_near():
        for mask in near:
            remote(y_send.at[places[mask]], causal.at[mask], n_sem.at[mask], {"seq": places[mask]}).start()

    def send_cross(phase, q):
        start, size = chunks[q]
        rows = pl.ds(start, size)
        for place in across_cut(phase):
            remote(
                y_send.at[place, rows], causal.at[half + seat, rows], x_sem.at[q], {"seq": place},
                gate.at[phase * len(chunks) + q],
            ).start()

    def gone(phase, q):
        spot = causal.at[0]
        remote(spot, spot, x_sem.at[q], {"seq": other}, gate.at[phase * len(chunks) + q]).wait_send()

    def slot(chan, mask):
        return mixed.at[chan, mask // 2, :, lanes(lax.rem(places[mask], 2))]

    def far_slot(chan, q):
        start, size = chunks[q]
        return mixed.at[chan, pl.ds(half // 2, half // 2), pl.ds(start, size)]

    def blend(place, y_rows, rows, target):
        cols = lanes(place)
        direct = skip[:, cols] * values[rows, cols].astype(jnp.float32)
        target[rows, :] = (gates[rows, cols].astype(jnp.float32) * (y_rows.astype(jnp.float32) + direct)).astype(
            jnp.bfloat16
        )

    def share(spot, a_sem, b_sem):
        remote(spot, spot, a_sem, {"chan": across}).start()
        remote(spot, spot, b_sem, {"chan": sibling}).start()

    def near_in(mask):
        if mask:
            spot = causal.at[mask]
            remote(spot, spot, n_sem.at[mask], {"seq": places[mask]}).wait_recv()
            blend(places[mask], causal[mask], every, slot(mine, mask))
        else:
            blend(me, y_send[me], every, slot(mine, mask))
        share(slot(mine, mask), an_sem.at[mask], bn_sem.at[mask])

    def cross_in(q):
        start, size = chunks[q]
        rows = pl.ds(start, size)
        spot = causal.at[pl.ds(half, half), rows]
        remote(spot, spot, x_sem.at[q], {"seq": other}).wait_recv()
        for t in range(half):
            blend(other + t, causal[half + t, rows], rows, mixed.at[mine, (half + t) // 2, :, lanes(t % 2)])
        share(far_slot(mine, q), ax_sem.at[q], bx_sem.at[q])

    def near_on(mask):
        spot = slot(across, mask)
        remote(spot, spot, an_sem.at[mask], {"chan": across}).wait_recv()
        remote(spot, spot, fn_sem.at[mask], {"chan": sibling}).start()

    def cross_on(q):
        spot = far_slot(across, q)
        remote(spot, spot, ax_sem.at[q], {"chan": across}).wait_recv()
        remote(spot, spot, fx_sem.at[q], {"chan": sibling}).start()

    def arrived(spot, sem):
        remote(spot, spot, sem, {"chan": sibling}).wait_recv()

    def project(ranks, start, size, pair, first, last):
        rows = pl.ds(start, size)

        def tile(n, _):
            cols = pl.ds(pl.multiple_of(n * 512, 512), 512)
            total = None
            for chan in pair:
                for rank in ranks:
                    source = places[2 * rank] // 2 if 2 * rank < half else other // 2 + rank - half // 2
                    deep = pl.ds(pl.multiple_of(chan * depth + source * 2 * LANES, 2 * LANES), 2 * LANES)
                    term = jnp.dot(mixed[chan, rank, rows], w[deep, cols], preferred_element_type=jnp.float32)
                    total = term if total is None else total + term
            if not first:
                total = total + acc[rows, cols]
            if last:
                out[rows, cols] = total.astype(out.dtype)
            else:
                acc[rows, cols] = total
            return 0

        lax.fori_loop(0, out.shape[1] // 512, tile, 0)

    close, far = range(half // 2), range(half // 2, half)
    masks = [0] + near

    def near_first():
        for mask in masks:
            arrived(slot(sibling, mask), bn_sem.at[mask])
        project(close, 0, block, (mine, sibling), True, False)

    def near_second():
        for mask in masks:
            arrived(slot(opposite, mask), fn_sem.at[mask])
        project(close, 0, block, (across, opposite), False, False)

    def cross_first(q):
        arrived(far_slot(sibling, q), bx_sem.at[q])
        project(far, *chunks[q], (mine, sibling), False, False)

    def cross_second(q):
        arrived(far_slot(opposite, q), fx_sem.at[q])
        project(far, *chunks[q], (across, opposite), False, True)

    transform(me)
    for mask in near:
        take_in(places[mask])
    backward_copy.wait()
    values_copy.wait()
    gates_copy.wait()

    @pl.when(upper == 0)
    def _():
        for rank in range(half // 2):
            produce(rank)
        send_near()
        near_in(0)
        for phase in range(half // 2):
            rank = half // 2 + phase
            take_in(2 * rank)
            take_in(2 * rank + 1)
            produce(rank)
            if phase == 0:
                send_cross(0, 0)
                send_cross(0, 1)

    @pl.when(upper == 1)
    def _():
        for rank in range(half // 2):
            take_in(2 * rank)
            take_in(2 * rank + 1)
            if rank == 0:
                produce(rank)
                send_cross(0, 0)
                send_cross(0, 1)
        for rank in range(half // 2, half):
            produce(rank)
        send_near()
        for rank in range(1, half // 2):
            produce(rank)
        near_in(0)

    w_copy.wait()
    gone(0, 0)
    gone(0, 1)
    send_cross(1, 0)
    send_cross(1, 1)
    for mask in near:
        near_in(mask)
    cross_in(0)
    cross_in(1)
    for mask in masks:
        near_on(mask)
    near_first()
    near_second()
    cross_on(0)
    cross_first(0)
    cross_on(1)
    cross_first(1)
    cross_second(0)
    cross_second(1)
    gone(1, 0)
    gone(1, 1)
    whole = w.at[pl.ds(0, (3 * (blocks - 1) + 3 * blocks - half) * block * LANES // w.shape[1])]
    remote(whole, whole, in_sem.at[0], {"chan": sibling}).wait_send()


def per_device_fused(blocks, chans, values, gates, filters, skip, w_out):
    block, width = values.shape
    forward, backward = tables(block)
    vmem = pl.BlockSpec(memory_space=pltpu.VMEM)
    hbm = pl.BlockSpec(memory_space=pl.ANY)
    out_width = w_out.shape[1]
    chunks = [(q * block // 2, block // 2) for q in range(2)]

    def sems(*shape):
        return pltpu.SemaphoreType.DMA(shape)

    half, pieces = blocks // 2, len(chunks)
    return pl.pallas_call(
        functools.partial(kernel, blocks, chans, chunks),
        out_shape=pltpu.VMEM((block, out_width), jnp.bfloat16),
        in_specs=[hbm, hbm, hbm, vmem, hbm, hbm, hbm],
        out_specs=vmem,
        scratch_shapes=[
            pltpu.VMEM((block, width), jnp.bfloat16),
            pltpu.VMEM((block, width), jnp.bfloat16),
            pltpu.VMEM((block, width), jnp.float32),
            pltpu.VMEM((block, width), jnp.bfloat16),
            pltpu.VMEM((blocks, block, 2 * LANES), jnp.bfloat16),
            pltpu.VMEM(forward.shape, jnp.bfloat16),
            pltpu.VMEM(backward.shape, jnp.bfloat16),
            pltpu.VMEM((blocks, 2 * block, 2 * LANES), jnp.float32),
            pltpu.VMEM((2, half, 2 * block, 2 * LANES), jnp.bfloat16),
            pltpu.VMEM((blocks, block, LANES), jnp.bfloat16),
            pltpu.VMEM((blocks, block, LANES), jnp.bfloat16),
            pltpu.VMEM((chans, half, block, 2 * LANES), jnp.bfloat16),
            pltpu.VMEM(w_out.shape, jnp.bfloat16),
            pltpu.VMEM((block, out_width), jnp.float32),
            sems(7), sems(1), sems(half), sems(blocks), sems(half), sems(pieces),
        ]
        + [sems(half), sems(pieces)] * 3,
        compiler_params=pltpu.CompilerParams(
            collective_id=0, has_side_effects=True, vmem_limit_bytes=56 * 2**20
        ),
    )(values, gates, filters, skip[None, :], jnp.asarray(forward), jnp.asarray(backward), w_out)


def per_device(mesh_shape, values, gates, filters, skip, w_out):
    blocks, chans = mesh_shape["seq"], mesh_shape["chan"]
    block, width = values.shape
    fits = (
        width == blocks * LANES and chans == 4 and blocks == 8 and block == 256
        and w_out.shape[0] == chans * width and w_out.shape[1] == 1024
    )
    if fits:
        return per_device_fused(blocks, chans, values, gates, filters, skip, w_out)
    return per_device_generic(values, gates, filters, skip, w_out)


def solution(mesh):
    placed = (P("seq", "chan"), P("seq", "chan"), P("seq", "chan"), P("chan"), P(None, "chan"))
    return jax.shard_map(
        functools.partial(per_device, dict(mesh.shape)),
        mesh=mesh, in_specs=placed, out_specs=P("seq", "chan"), check_vma=False,
    )
```

```python
import functools
import math

import jax
import jax.numpy as jnp
import numpy as np
from jax import lax
from jax.experimental import pallas as pl
from jax.experimental.pallas import tpu as pltpu
from jax.sharding import PartitionSpec as P

LANES = 128
STRIP = 16
MESH = pl.DeviceIdType.MESH


def product(form, left, right):
    return jnp.einsum(
        form, left, right, precision=lax.Precision.HIGHEST, preferred_element_type=jnp.float32
    )


def phase(first_count, second_count, modulus):
    left = lax.iota(jnp.int32, first_count)[:, None]
    right = lax.iota(jnp.int32, second_count)[None, :]
    angle = (left * right % modulus).astype(jnp.float32) * (2.0 * math.pi / modulus)
    return (jnp.cos(angle), jnp.sin(angle))


def spectral_conv(chan_values, chan_filter):
    nchan = chan_values.shape[0]
    length = chan_values.shape[1]
    summed = 2 * length
    columns = 128
    row_count = summed // columns
    half_rows = row_count // 2
    cos_rows, sin_rows = phase(row_count, half_rows, row_count)
    cos_twist, sin_twist = phase(row_count, columns, summed)
    cos_cols, sin_cols = phase(columns, columns, columns)
    cos_back, sin_back = phase(half_rows, row_count, row_count)

    def forward(signal):
        grid = signal.astype(jnp.float32).reshape(nchan, half_rows, columns)
        real_a = product("kn,cna->cka", cos_rows, grid)
        imag_a = -product("kn,cna->cka", sin_rows, grid)
        real_b = real_a * cos_twist + imag_a * sin_twist
        imag_b = imag_a * cos_twist - real_a * sin_twist
        real_c = product("cka,am->ckm", real_b, cos_cols) + product("cka,am->ckm", imag_b, sin_cols)
        imag_c = product("cka,am->ckm", imag_b, cos_cols) - product("cka,am->ckm", real_b, sin_cols)
        return (real_c, imag_c)

    real_v, imag_v = forward(chan_values)
    real_h, imag_h = forward(chan_filter)
    real_p = real_v * real_h - imag_v * imag_h
    imag_p = real_v * imag_h + imag_v * real_h
    real_d = product("ckm,ma->cka", real_p, cos_cols) - product("ckm,ma->cka", imag_p, sin_cols)
    imag_d = product("ckm,ma->cka", imag_p, cos_cols) + product("ckm,ma->cka", real_p, sin_cols)
    real_e = real_d * cos_twist - imag_d * sin_twist
    imag_e = imag_d * cos_twist + real_d * sin_twist
    result = product("nk,cka->cna", cos_back, real_e) - product("nk,cka->cna", sin_back, imag_e)
    return (result * (1.0 / summed)).reshape(nchan, length).astype(jnp.bfloat16)


def per_device_generic(values, gates, filters, skip, w_out):
    value_trans = values.T
    filter_trans = filters.T
    chan_values = lax.all_to_all(value_trans, "seq", split_axis=0, concat_axis=1, tiled=True)
    chan_filter = lax.all_to_all(filter_trans, "seq", split_axis=0, concat_axis=1, tiled=True)
    convolved = spectral_conv(chan_values, chan_filter)
    causal_trans = lax.all_to_all(convolved, "seq", split_axis=1, concat_axis=0, tiled=True)
    causal = causal_trans.T
    mixed = (
        gates.astype(jnp.float32)
        * (causal.astype(jnp.float32) + skip[None, :] * values.astype(jnp.float32))
    ).astype(jnp.bfloat16)
    projected = jnp.dot(
        lax.all_gather(mixed, "chan", axis=1, tiled=True), w_out, preferred_element_type=jnp.float32
    )
    return projected.astype(jnp.bfloat16)


def split(x):
    high = x.astype(jnp.bfloat16)
    return high, (x - high.astype(jnp.float32)).astype(jnp.bfloat16)


def tables(block):
    index = np.arange(block)
    angle = np.pi * (np.outer(4 * index + 1, index) % (4 * block)) / (2 * block)
    whole = np.concatenate([np.cos(angle), -np.sin(angle)]).astype(np.float32)
    high = whole.astype(jnp.bfloat16)
    both = np.stack([high, (whole - high.astype(np.float32)).astype(jnp.bfloat16)])
    back = (both.astype(np.float32) / block).astype(jnp.bfloat16)
    return both, np.ascontiguousarray(back.transpose(0, 2, 1))


def kernel(
    blocks, chans, chunks,
    values_hbm, gates_hbm, filters_hbm, skip, forward_hbm, backward_hbm, w_hbm,
    out,
    values, gates, filters, h_send, got, forward, backward, spec, y, y_send, causal, mixed, w, acc,
    relay, l_sem, sent, gate, in_sem, n_sem, x_sem, an_sem, ax_sem, bn_sem, bx_sem, fn_sem, fx_sem,
):
    me = lax.axis_index("seq")
    mine = lax.axis_index("chan")
    block = values.shape[0]
    depth = values.shape[1]
    half = blocks // 2
    left, right = pl.ds(0, LANES), pl.ds(LANES, LANES)
    every = pl.ds(0, block)
    near = list(range(1, half))
    upper = me // half
    seat = lax.rem(me, half)
    other = half - half * upper
    odd = lax.rem(me, 2)

    def lanes(position):
        return pl.ds(pl.multiple_of(position * LANES, LANES), LANES)

    def partner(mask):
        place = me
        bit = 1
        while bit < half:
            if mask & bit:
                place = place + bit - 2 * bit * lax.rem(place // bit, 2)
            bit *= 2
        return place

    places = [partner(mask) for mask in range(half)]

    local = [
        pltpu.make_async_copy(source, target, l_sem.at[i])
        for i, (source, target) in enumerate((
            (filters_hbm, filters), (values_hbm, values), (values_hbm.at[:, lanes(me)], got.at[me, :, left]),
            (forward_hbm, forward), (backward_hbm, backward), (gates_hbm, gates), (w_hbm, w),
        ))
    ]
    filters_copy, values_copy, own_copy, forward_copy, backward_copy, gates_copy, w_copy = local
    for copy in local:
        copy.start()

    sibling = mine + 1 - 2 * lax.rem(mine, 2)
    across = lax.rem(mine + 2, chans)
    opposite = lax.rem(sibling + 2, chans)
    level = me // 2
    levels = blocks // 2
    inside = lax.rem((level + 1) // 2, 2)
    turned = me + 1 - 2 * odd
    barrier = pltpu.get_barrier_semaphore()

    def greet(sem):
        pl.semaphore_signal(sem, inc=1, device_id={"seq": turned}, device_id_type=MESH)

        @pl.when(level > 0)
        def _():
            pl.semaphore_signal(sem, inc=1, device_id={"seq": me - 2}, device_id_type=MESH)

        @pl.when(level < levels - 1)
        def _():
            pl.semaphore_signal(sem, inc=1, device_id={"seq": me + 2}, device_id_type=MESH)

    greet(barrier)
    for chan in (sibling, across):
        pl.semaphore_signal(barrier, inc=1, device_id={"chan": chan}, device_id_type=MESH)
    filters_copy.wait()
    h_send[...] = filters[...].astype(jnp.bfloat16)
    pl.semaphore_wait(barrier, 4 + inside)
    greet(relay.at[0])

    def remote(source, target, sem, where, out_sem=None):
        return pltpu.make_async_remote_copy(
            src_ref=source, dst_ref=target, send_sem=sent.at[0] if out_sem is None else out_sem, recv_sem=sem,
            device_id=where, device_id_type=MESH,
        )

    def across_cut(phase):
        return [other + 2 * phase + odd, other + 2 * phase + 1 - odd]

    def send_in(place):
        remote(values_hbm.at[:, lanes(place)], got.at[me, :, left], in_sem.at[me], {"seq": place}).start()
        remote(h_send.at[:, lanes(place)], got.at[me, :, right], in_sem.at[me], {"seq": place}).start()

    first, second = across_cut(upper), across_cut(1 - upper)

    @pl.when(inside == 1)
    def _():
        send_in(first[0])

    @pl.when(inside == 0)
    def _():
        send_in(places[2])
        send_in(places[1])

    for stage in range(1, 4):
        pl.semaphore_wait(relay.at[stage - 1], 2 + inside)
        if stage < 3:
            greet(relay.at[stage])
        early = {1: [first[1], second[0]], 2: [second[1], places[2], places[1]], 3: [places[3]]}[stage]
        late = {1: [first[0], places[3]], 2: [first[1], second[0]], 3: [second[1]]}[stage]

        @pl.when(inside == 1)
        def _():
            for place in early:
                send_in(place)

        @pl.when(inside == 0)
        def _():
            for place in late:
                send_in(place)

    got[me, :, LANES:] = h_send[:, lanes(me)]
    own_copy.wait()
    forward_copy.wait()

    def transform(place):
        x = got[place]
        spec[place] = jnp.dot(forward[0], x, preferred_element_type=jnp.float32) + jnp.dot(
            forward[1], x, preferred_element_type=jnp.float32
        )

    def take_in(place):
        spot = got.at[place]
        remote(spot, spot, in_sem.at[place], {"seq": other}).wait_recv()
        transform(place)

    def combine(pair):
        def body(strip, _):
            parts = []
            for part in range(STRIP // 8):
                re_rows = pl.ds(pl.multiple_of(strip * STRIP + 8 * part, 8), 8)
                im_rows = pl.ds(pl.multiple_of(block + strip * STRIP + 8 * part, 8), 8)
                count = pair[-1] + 1
                v = [(spec[n, re_rows, :LANES], spec[n, im_rows, :LANES]) for n in range(count)]
                h = [(spec[n, re_rows, LANES:], spec[n, im_rows, LANES:]) for n in range(count)]
                g = [h[0]] + [(h[n][0] - h[n - 1][1], h[n][1] + h[n - 1][0]) for n in range(1, count)]
                sums = []
                for k in pair:
                    re = im = None
                    for n in range(k + 1):
                        (a, b), (c, d) = v[n], g[k - n]
                        re_term, im_term = a * c - b * d, a * d + b * c
                        re = re_term if re is None else re + re_term
                        im = im_term if im is None else im + im_term
                    sums.append((re, im))
                parts.append(sums)
            for i in (0, 1):
                for which in (0, 1):
                    high, low = split(jnp.concatenate([sums[i][which] for sums in parts], axis=0))
                    rows = pl.ds(pl.multiple_of(which * block + strip * STRIP, STRIP), STRIP)
                    y[0, pair[0] // 2, rows, i * LANES : (i + 1) * LANES] = high
                    y[1, pair[0] // 2, rows, i * LANES : (i + 1) * LANES] = low
            return 0

        lax.fori_loop(0, block // STRIP, body, 0)

    def produce(rank):
        pair = (2 * rank, 2 * rank + 1)
        combine(pair)
        high, low = y[0, rank], y[1, rank]
        x = (
            jnp.dot(backward[0], high, preferred_element_type=jnp.float32)
            + jnp.dot(backward[1], high, preferred_element_type=jnp.float32)
            + jnp.dot(backward[0], low, preferred_element_type=jnp.float32)
        ).astype(jnp.bfloat16)
        y_send[pair[0]] = x[:, :LANES]
        y_send[pair[1]] = x[:, LANES:]

    def send_near():
        for mask in near:
            remote(y_send.at[places[mask]], causal.at[mask], n_sem.at[mask], {"seq": places[mask]}).start()

    def send_cross(phase, q):
        start, size = chunks[q]
        rows = pl.ds(start, size)
        for place in across_cut(phase):
            remote(
                y_send.at[place, rows], causal.at[half + seat, rows], x_sem.at[q], {"seq": place},
                gate.at[phase * len(chunks) + q],
            ).start()

    def gone(phase, q):
        spot = causal.at[0]
        remote(spot, spot, x_sem.at[q], {"seq": other}, gate.at[phase * len(chunks) + q]).wait_send()

    def slot(chan, mask):
        return mixed.at[chan, mask // 2, :, lanes(lax.rem(places[mask], 2))]

    def far_slot(chan, q):
        start, size = chunks[q]
        return mixed.at[chan, pl.ds(half // 2, half // 2), pl.ds(start, size)]

    def blend(place, y_rows, rows, target):
        cols = lanes(place)
        direct = skip[:, cols] * values[rows, cols].astype(jnp.float32)
        target[rows, :] = (gates[rows, cols].astype(jnp.float32) * (y_rows.astype(jnp.float32) + direct)).astype(
            jnp.bfloat16
        )

    def share(spot, a_sem, b_sem):
        remote(spot, spot, a_sem, {"chan": across}).start()
        remote(spot, spot, b_sem, {"chan": sibling}).start()

    def near_in(mask):
        if mask:
            spot = causal.at[mask]
            remote(spot, spot, n_sem.at[mask], {"seq": places[mask]}).wait_recv()
            blend(places[mask], causal[mask], every, slot(mine, mask))
        else:
            blend(me, y_send[me], every, slot(mine, mask))
        share(slot(mine, mask), an_sem.at[mask], bn_sem.at[mask])

    def cross_in(q):
        start, size = chunks[q]
        rows = pl.ds(start, size)
        spot = causal.at[pl.ds(half, half), rows]
        remote(spot, spot, x_sem.at[q], {"seq": other}).wait_recv()
        for t in range(half):
            blend(other + t, causal[half + t, rows], rows, mixed.at[mine, (half + t) // 2, :, lanes(t % 2)])
        share(far_slot(mine, q), ax_sem.at[q], bx_sem.at[q])

    def near_on(mask):
        spot = slot(across, mask)
        remote(spot, spot, an_sem.at[mask], {"chan": across}).wait_recv()
        remote(spot, spot, fn_sem.at[mask], {"chan": sibling}).start()

    def cross_on(q):
        spot = far_slot(across, q)
        remote(spot, spot, ax_sem.at[q], {"chan": across}).wait_recv()
        remote(spot, spot, fx_sem.at[q], {"chan": sibling}).start()

    def arrived(spot, sem):
        remote(spot, spot, sem, {"chan": sibling}).wait_recv()

    def project(ranks, start, size, pair, first, last):
        rows = pl.ds(start, size)

        def tile(n, _):
            cols = pl.ds(pl.multiple_of(n * 512, 512), 512)
            total = None
            for chan in pair:
                for rank in ranks:
                    source = places[2 * rank] // 2 if 2 * rank < half else other // 2 + rank - half // 2
                    deep = pl.ds(pl.multiple_of(chan * depth + source * 2 * LANES, 2 * LANES), 2 * LANES)
                    term = jnp.dot(mixed[chan, rank, rows], w[deep, cols], preferred_element_type=jnp.float32)
                    total = term if total is None else total + term
            if not first:
                total = total + acc[rows, cols]
            if last:
                out[rows, cols] = total.astype(out.dtype)
            else:
                acc[rows, cols] = total
            return 0

        lax.fori_loop(0, out.shape[1] // 512, tile, 0)

    close, far = range(half // 2), range(half // 2, half)
    masks = [0] + near

    def near_first():
        for mask in masks:
            arrived(slot(sibling, mask), bn_sem.at[mask])
        project(close, 0, block, (mine, sibling), True, False)

    def near_second():
        for mask in masks:
            arrived(slot(opposite, mask), fn_sem.at[mask])
        project(close, 0, block, (across, opposite), False, False)

    def cross_first(q):
        arrived(far_slot(sibling, q), bx_sem.at[q])
        project(far, *chunks[q], (mine, sibling), False, False)

    def cross_second(q):
        arrived(far_slot(opposite, q), fx_sem.at[q])
        project(far, *chunks[q], (across, opposite), False, True)

    transform(me)
    for mask in near:
        take_in(places[mask])
    backward_copy.wait()
    values_copy.wait()
    gates_copy.wait()

    @pl.when(upper == 0)
    def _():
        for rank in range(half // 2):
            produce(rank)
        send_near()
        near_in(0)
        for phase in range(half // 2):
            rank = half // 2 + phase
            take_in(2 * rank)
            take_in(2 * rank + 1)
            produce(rank)
            if phase == 0:
                send_cross(0, 0)
                send_cross(0, 1)

    @pl.when(upper == 1)
    def _():
        for rank in range(half // 2):
            take_in(2 * rank)
            take_in(2 * rank + 1)
            if rank == 0:
                produce(rank)
                send_cross(0, 0)
                send_cross(0, 1)
        for rank in range(half // 2, half):
            produce(rank)
        send_near()
        for rank in range(1, half // 2):
            produce(rank)
        near_in(0)

    w_copy.wait()
    gone(0, 0)
    gone(0, 1)
    send_cross(1, 0)
    send_cross(1, 1)
    for mask in near:
        near_in(mask)
    cross_in(0)
    cross_in(1)
    for mask in masks:
        near_on(mask)
    near_first()
    near_second()
    cross_on(0)
    cross_first(0)
    cross_on(1)
    cross_first(1)
    cross_second(0)
    cross_second(1)
    gone(1, 0)
    gone(1, 1)
    whole = w.at[pl.ds(0, (3 * (blocks - 1) + 3 * blocks - half) * block * LANES // w.shape[1])]
    remote(whole, whole, in_sem.at[0], {"chan": sibling}).wait_send()


def per_device_fused(blocks, chans, values, gates, filters, skip, w_out):
    block, width = values.shape
    forward, backward = tables(block)
    vmem = pl.BlockSpec(memory_space=pltpu.VMEM)
    hbm = pl.BlockSpec(memory_space=pl.ANY)
    out_width = w_out.shape[1]
    chunks = [(q * block // 2, block // 2) for q in range(2)]

    def sems(*shape):
        return pltpu.SemaphoreType.DMA(shape)

    half, pieces = blocks // 2, len(chunks)
    return pl.pallas_call(
        functools.partial(kernel, blocks, chans, chunks),
        out_shape=pltpu.VMEM((block, out_width), jnp.bfloat16),
        in_specs=[hbm, hbm, hbm, vmem, hbm, hbm, hbm],
        out_specs=vmem,
        scratch_shapes=[
            pltpu.VMEM((block, width), jnp.bfloat16),
            pltpu.VMEM((block, width), jnp.bfloat16),
            pltpu.VMEM((block, width), jnp.float32),
            pltpu.VMEM((block, width), jnp.bfloat16),
            pltpu.VMEM((blocks, block, 2 * LANES), jnp.bfloat16),
            pltpu.VMEM(forward.shape, jnp.bfloat16),
            pltpu.VMEM(backward.shape, jnp.bfloat16),
            pltpu.VMEM((blocks, 2 * block, 2 * LANES), jnp.float32),
            pltpu.VMEM((2, half, 2 * block, 2 * LANES), jnp.bfloat16),
            pltpu.VMEM((blocks, block, LANES), jnp.bfloat16),
            pltpu.VMEM((blocks, block, LANES), jnp.bfloat16),
            pltpu.VMEM((chans, half, block, 2 * LANES), jnp.bfloat16),
            pltpu.VMEM(w_out.shape, jnp.bfloat16),
            pltpu.VMEM((block, out_width), jnp.float32),
            pltpu.SemaphoreType.REGULAR((3,)), sems(7), sems(1), sems(half), sems(blocks), sems(half), sems(pieces),
        ]
        + [sems(half), sems(pieces)] * 3,
        compiler_params=pltpu.CompilerParams(
            collective_id=0, has_side_effects=True, vmem_limit_bytes=56 * 2**20
        ),
    )(values, gates, filters, skip[None, :], jnp.asarray(forward), jnp.asarray(backward), w_out)


def per_device(mesh_shape, values, gates, filters, skip, w_out):
    blocks, chans = mesh_shape["seq"], mesh_shape["chan"]
    block, width = values.shape
    fits = (
        width == blocks * LANES and chans == 4 and blocks == 8 and block == 256
        and w_out.shape[0] == chans * width and w_out.shape[1] == 1024
    )
    if fits:
        return per_device_fused(blocks, chans, values, gates, filters, skip, w_out)
    return per_device_generic(values, gates, filters, skip, w_out)


def solution(mesh):
    placed = (P("seq", "chan"), P("seq", "chan"), P("seq", "chan"), P("chan"), P(None, "chan"))
    return jax.shard_map(
        functools.partial(per_device, dict(mesh.shape)),
        mesh=mesh, in_specs=placed, out_specs=P("seq", "chan"), check_vma=False,
    )
```

```python
import functools
import math

import jax
import jax.numpy as jnp
import numpy as np
from jax import lax
from jax.experimental import pallas as pl
from jax.experimental.pallas import tpu as pltpu
from jax.sharding import PartitionSpec as P

LANES = 128
STRIP = 16
MESH = pl.DeviceIdType.MESH


def product(form, left, right):
    return jnp.einsum(
        form, left, right, precision=lax.Precision.HIGHEST, preferred_element_type=jnp.float32
    )


def phase(first_count, second_count, modulus):
    left = lax.iota(jnp.int32, first_count)[:, None]
    right = lax.iota(jnp.int32, second_count)[None, :]
    angle = (left * right % modulus).astype(jnp.float32) * (2.0 * math.pi / modulus)
    return (jnp.cos(angle), jnp.sin(angle))


def spectral_conv(chan_values, chan_filter):
    nchan = chan_values.shape[0]
    length = chan_values.shape[1]
    summed = 2 * length
    columns = 128
    row_count = summed // columns
    half_rows = row_count // 2
    cos_rows, sin_rows = phase(row_count, half_rows, row_count)
    cos_twist, sin_twist = phase(row_count, columns, summed)
    cos_cols, sin_cols = phase(columns, columns, columns)
    cos_back, sin_back = phase(half_rows, row_count, row_count)

    def forward(signal):
        grid = signal.astype(jnp.float32).reshape(nchan, half_rows, columns)
        real_a = product("kn,cna->cka", cos_rows, grid)
        imag_a = -product("kn,cna->cka", sin_rows, grid)
        real_b = real_a * cos_twist + imag_a * sin_twist
        imag_b = imag_a * cos_twist - real_a * sin_twist
        real_c = product("cka,am->ckm", real_b, cos_cols) + product("cka,am->ckm", imag_b, sin_cols)
        imag_c = product("cka,am->ckm", imag_b, cos_cols) - product("cka,am->ckm", real_b, sin_cols)
        return (real_c, imag_c)

    real_v, imag_v = forward(chan_values)
    real_h, imag_h = forward(chan_filter)
    real_p = real_v * real_h - imag_v * imag_h
    imag_p = real_v * imag_h + imag_v * real_h
    real_d = product("ckm,ma->cka", real_p, cos_cols) - product("ckm,ma->cka", imag_p, sin_cols)
    imag_d = product("ckm,ma->cka", imag_p, cos_cols) + product("ckm,ma->cka", real_p, sin_cols)
    real_e = real_d * cos_twist - imag_d * sin_twist
    imag_e = imag_d * cos_twist + real_d * sin_twist
    result = product("nk,cka->cna", cos_back, real_e) - product("nk,cka->cna", sin_back, imag_e)
    return (result * (1.0 / summed)).reshape(nchan, length).astype(jnp.bfloat16)


def per_device_generic(values, gates, filters, skip, w_out):
    value_trans = values.T
    filter_trans = filters.T
    chan_values = lax.all_to_all(value_trans, "seq", split_axis=0, concat_axis=1, tiled=True)
    chan_filter = lax.all_to_all(filter_trans, "seq", split_axis=0, concat_axis=1, tiled=True)
    convolved = spectral_conv(chan_values, chan_filter)
    causal_trans = lax.all_to_all(convolved, "seq", split_axis=1, concat_axis=0, tiled=True)
    causal = causal_trans.T
    mixed = (
        gates.astype(jnp.float32)
        * (causal.astype(jnp.float32) + skip[None, :] * values.astype(jnp.float32))
    ).astype(jnp.bfloat16)
    projected = jnp.dot(
        lax.all_gather(mixed, "chan", axis=1, tiled=True), w_out, preferred_element_type=jnp.float32
    )
    return projected.astype(jnp.bfloat16)


def split(x):
    high = x.astype(jnp.bfloat16)
    return high, (x - high.astype(jnp.float32)).astype(jnp.bfloat16)


def tables(block):
    index = np.arange(block)
    angle = np.pi * (np.outer(4 * index + 1, index) % (4 * block)) / (2 * block)
    whole = np.concatenate([np.cos(angle), -np.sin(angle)]).astype(np.float32)
    high = whole.astype(jnp.bfloat16)
    both = np.stack([high, (whole - high.astype(np.float32)).astype(jnp.bfloat16)])
    back = (both.astype(np.float32) / block).astype(jnp.bfloat16)
    return both, np.ascontiguousarray(back.transpose(0, 2, 1))


def kernel(
    blocks, chans, chunks,
    values_hbm, gates_hbm, filters_hbm, skip, forward_hbm, backward_hbm, w_hbm,
    out,
    values, gates, filters, h_send, got, forward, backward, spec, y, y_send, causal, mixed, w, acc,
    relay, l_sem, sent, gate, in_sem, n_sem, x_sem, an_sem, ax_sem, bn_sem, bx_sem, fn_sem, fx_sem,
):
    me = lax.axis_index("seq")
    mine = lax.axis_index("chan")
    block = values.shape[0]
    depth = values.shape[1]
    half = blocks // 2
    left, right = pl.ds(0, LANES), pl.ds(LANES, LANES)
    every = pl.ds(0, block)
    near = list(range(1, half))
    upper = me // half
    seat = lax.rem(me, half)
    other = half - half * upper
    odd = lax.rem(me, 2)

    def lanes(position):
        return pl.ds(pl.multiple_of(position * LANES, LANES), LANES)

    def partner(mask):
        place = me
        bit = 1
        while bit < half:
            if mask & bit:
                place = place + bit - 2 * bit * lax.rem(place // bit, 2)
            bit *= 2
        return place

    places = [partner(mask) for mask in range(half)]

    local = [
        pltpu.make_async_copy(source, target, l_sem.at[i])
        for i, (source, target) in enumerate((
            (filters_hbm, filters), (values_hbm, values), (values_hbm.at[:, lanes(me)], got.at[me, :, left]),
            (forward_hbm, forward), (backward_hbm, backward), (gates_hbm, gates), (w_hbm, w),
        ))
    ]
    filters_copy, values_copy, own_copy, forward_copy, backward_copy, gates_copy, w_copy = local
    for copy in local:
        copy.start()

    sibling = mine + 1 - 2 * lax.rem(mine, 2)
    across = lax.rem(mine + 2, chans)
    opposite = lax.rem(sibling + 2, chans)
    level = me // 2
    levels = blocks // 2
    inside = lax.rem((level + 1) // 2, 2)
    turned = me + 1 - 2 * odd
    barrier = pltpu.get_barrier_semaphore()

    def greet(sem):
        pl.semaphore_signal(sem, inc=1, device_id={"seq": turned}, device_id_type=MESH)

        @pl.when(level > 0)
        def _():
            pl.semaphore_signal(sem, inc=1, device_id={"seq": me - 2}, device_id_type=MESH)

        @pl.when(level < levels - 1)
        def _():
            pl.semaphore_signal(sem, inc=1, device_id={"seq": me + 2}, device_id_type=MESH)

    greet(barrier)
    for chan in (sibling, across):
        pl.semaphore_signal(barrier, inc=1, device_id={"chan": chan}, device_id_type=MESH)
    filters_copy.wait()
    h_send[...] = filters[...].astype(jnp.bfloat16)
    pl.semaphore_wait(barrier, 4 + inside)
    greet(relay.at[0])

    def remote(source, target, sem, where, out_sem=None):
        return pltpu.make_async_remote_copy(
            src_ref=source, dst_ref=target, send_sem=sent.at[0] if out_sem is None else out_sem, recv_sem=sem,
            device_id=where, device_id_type=MESH,
        )

    def across_cut(phase):
        return [other + 2 * phase + odd, other + 2 * phase + 1 - odd]

    def send_in(place):
        remote(values_hbm.at[:, lanes(place)], got.at[me, :, left], in_sem.at[me], {"seq": place}).start()
        remote(h_send.at[:, lanes(place)], got.at[me, :, right], in_sem.at[me], {"seq": place}).start()

    first, second = across_cut(upper), across_cut(1 - upper)

    @pl.when(inside == 1)
    def _():
        send_in(first[0])

    @pl.when(inside == 0)
    def _():
        send_in(places[2])
        send_in(places[1])

    for stage in range(1, 4):
        pl.semaphore_wait(relay.at[stage - 1], 2 + inside)
        if stage < 3:
            greet(relay.at[stage])
        plans = (
            (1, 0, {1: [first[1], second[0]], 2: [second[1], places[2], places[1]], 3: [places[3]]}),
            (0, 0, {1: [first[0], places[3]], 2: [first[1], second[0]], 3: [second[1]]}),
            (1, 1, {1: [second[0]], 2: [first[1], second[1], places[2], places[1]], 3: [places[3]]}),
            (0, 1, {1: [first[0], places[3]], 2: [second[0], first[1]], 3: [second[1]]}),
        )
        for within, side, plan in plans:

            @pl.when(jnp.logical_and(inside == within, upper == side))
            def _():
                for place in plan[stage]:
                    send_in(place)

    got[me, :, LANES:] = h_send[:, lanes(me)]
    own_copy.wait()
    forward_copy.wait()

    def transform(place):
        x = got[place]
        spec[place] = jnp.dot(forward[0], x, preferred_element_type=jnp.float32) + jnp.dot(
            forward[1], x, preferred_element_type=jnp.float32
        )

    def take_in(place):
        spot = got.at[place]
        remote(spot, spot, in_sem.at[place], {"seq": other}).wait_recv()
        transform(place)

    def combine(pair):
        def body(strip, _):
            parts = []
            for part in range(STRIP // 8):
                re_rows = pl.ds(pl.multiple_of(strip * STRIP + 8 * part, 8), 8)
                im_rows = pl.ds(pl.multiple_of(block + strip * STRIP + 8 * part, 8), 8)
                count = pair[-1] + 1
                v = [(spec[n, re_rows, :LANES], spec[n, im_rows, :LANES]) for n in range(count)]
                h = [(spec[n, re_rows, LANES:], spec[n, im_rows, LANES:]) for n in range(count)]
                g = [h[0]] + [(h[n][0] - h[n - 1][1], h[n][1] + h[n - 1][0]) for n in range(1, count)]
                sums = []
                for k in pair:
                    re = im = None
                    for n in range(k + 1):
                        (a, b), (c, d) = v[n], g[k - n]
                        re_term, im_term = a * c - b * d, a * d + b * c
                        re = re_term if re is None else re + re_term
                        im = im_term if im is None else im + im_term
                    sums.append((re, im))
                parts.append(sums)
            for i in (0, 1):
                for which in (0, 1):
                    high, low = split(jnp.concatenate([sums[i][which] for sums in parts], axis=0))
                    rows = pl.ds(pl.multiple_of(which * block + strip * STRIP, STRIP), STRIP)
                    y[0, pair[0] // 2, rows, i * LANES : (i + 1) * LANES] = high
                    y[1, pair[0] // 2, rows, i * LANES : (i + 1) * LANES] = low
            return 0

        lax.fori_loop(0, block // STRIP, body, 0)

    def produce(rank):
        pair = (2 * rank, 2 * rank + 1)
        combine(pair)
        high, low = y[0, rank], y[1, rank]
        x = (
            jnp.dot(backward[0], high, preferred_element_type=jnp.float32)
            + jnp.dot(backward[1], high, preferred_element_type=jnp.float32)
            + jnp.dot(backward[0], low, preferred_element_type=jnp.float32)
        ).astype(jnp.bfloat16)
        y_send[pair[0]] = x[:, :LANES]
        y_send[pair[1]] = x[:, LANES:]

    def send_near():
        for mask in near:
            remote(y_send.at[places[mask]], causal.at[mask], n_sem.at[mask], {"seq": places[mask]}).start()

    def send_cross(phase, q):
        start, size = chunks[q]
        rows = pl.ds(start, size)
        for place in across_cut(phase):
            remote(
                y_send.at[place, rows], causal.at[half + seat, rows], x_sem.at[q], {"seq": place},
                gate.at[phase * len(chunks) + q],
            ).start()

    def gone(phase, q):
        spot = causal.at[0]
        remote(spot, spot, x_sem.at[q], {"seq": other}, gate.at[phase * len(chunks) + q]).wait_send()

    def slot(chan, mask):
        return mixed.at[chan, mask // 2, :, lanes(lax.rem(places[mask], 2))]

    def far_slot(chan, q):
        start, size = chunks[q]
        return mixed.at[chan, pl.ds(half // 2, half // 2), pl.ds(start, size)]

    def blend(place, y_rows, rows, target):
        cols = lanes(place)
        direct = skip[:, cols] * values[rows, cols].astype(jnp.float32)
        target[rows, :] = (gates[rows, cols].astype(jnp.float32) * (y_rows.astype(jnp.float32) + direct)).astype(
            jnp.bfloat16
        )

    def share(spot, a_sem, b_sem):
        remote(spot, spot, a_sem, {"chan": across}).start()
        remote(spot, spot, b_sem, {"chan": sibling}).start()

    def near_in(mask):
        if mask:
            spot = causal.at[mask]
            remote(spot, spot, n_sem.at[mask], {"seq": places[mask]}).wait_recv()
            blend(places[mask], causal[mask], every, slot(mine, mask))
        else:
            blend(me, y_send[me], every, slot(mine, mask))
        share(slot(mine, mask), an_sem.at[mask], bn_sem.at[mask])

    def cross_in(q):
        start, size = chunks[q]
        rows = pl.ds(start, size)
        spot = causal.at[pl.ds(half, half), rows]
        remote(spot, spot, x_sem.at[q], {"seq": other}).wait_recv()
        for t in range(half):
            blend(other + t, causal[half + t, rows], rows, mixed.at[mine, (half + t) // 2, :, lanes(t % 2)])
        share(far_slot(mine, q), ax_sem.at[q], bx_sem.at[q])

    def near_on(mask):
        spot = slot(across, mask)
        remote(spot, spot, an_sem.at[mask], {"chan": across}).wait_recv()
        remote(spot, spot, fn_sem.at[mask], {"chan": sibling}).start()

    def cross_on(q):
        spot = far_slot(across, q)
        remote(spot, spot, ax_sem.at[q], {"chan": across}).wait_recv()
        remote(spot, spot, fx_sem.at[q], {"chan": sibling}).start()

    def arrived(spot, sem):
        remote(spot, spot, sem, {"chan": sibling}).wait_recv()

    def project(ranks, start, size, pair, first, last):
        rows = pl.ds(start, size)

        def tile(n, _):
            cols = pl.ds(pl.multiple_of(n * 512, 512), 512)
            total = None
            for chan in pair:
                for rank in ranks:
                    source = places[2 * rank] // 2 if 2 * rank < half else other // 2 + rank - half // 2
                    deep = pl.ds(pl.multiple_of(chan * depth + source * 2 * LANES, 2 * LANES), 2 * LANES)
                    term = jnp.dot(mixed[chan, rank, rows], w[deep, cols], preferred_element_type=jnp.float32)
                    total = term if total is None else total + term
            if not first:
                total = total + acc[rows, cols]
            if last:
                out[rows, cols] = total.astype(out.dtype)
            else:
                acc[rows, cols] = total
            return 0

        lax.fori_loop(0, out.shape[1] // 512, tile, 0)

    close, far = range(half // 2), range(half // 2, half)
    masks = [0] + near

    def near_first():
        for mask in masks:
            arrived(slot(sibling, mask), bn_sem.at[mask])
        project(close, 0, block, (mine, sibling), True, False)

    def near_second():
        for mask in masks:
            arrived(slot(opposite, mask), fn_sem.at[mask])
        project(close, 0, block, (across, opposite), False, False)

    def cross_first(q):
        arrived(far_slot(sibling, q), bx_sem.at[q])
        project(far, *chunks[q], (mine, sibling), False, False)

    def cross_second(q):
        arrived(far_slot(opposite, q), fx_sem.at[q])
        project(far, *chunks[q], (across, opposite), False, True)

    transform(me)
    for mask in near:
        take_in(places[mask])
    backward_copy.wait()
    values_copy.wait()
    gates_copy.wait()

    @pl.when(upper == 0)
    def _():
        for rank in range(half // 2):
            produce(rank)
        send_near()
        near_in(0)
        for phase in range(half // 2):
            rank = half // 2 + phase
            take_in(2 * rank)
            take_in(2 * rank + 1)
            produce(rank)
            if phase == 0:
                send_cross(0, 0)
                send_cross(0, 1)

    @pl.when(upper == 1)
    def _():
        for rank in range(half // 2):
            take_in(2 * rank)
            take_in(2 * rank + 1)
            if rank == 0:
                produce(rank)
                send_cross(0, 0)
                send_cross(0, 1)
        for rank in range(half // 2, half):
            produce(rank)
        send_near()
        for rank in range(1, half // 2):
            produce(rank)
        near_in(0)

    w_copy.wait()
    gone(0, 0)
    gone(0, 1)
    send_cross(1, 0)
    send_cross(1, 1)
    for mask in near:
        near_in(mask)
    cross_in(0)
    cross_in(1)
    for mask in masks:
        near_on(mask)
    near_first()
    near_second()
    cross_on(0)
    cross_first(0)
    cross_on(1)
    cross_first(1)
    cross_second(0)
    cross_second(1)
    gone(1, 0)
    gone(1, 1)
    whole = w.at[pl.ds(0, (3 * (blocks - 1) + 3 * blocks - half) * block * LANES // w.shape[1])]
    remote(whole, whole, in_sem.at[0], {"chan": sibling}).wait_send()


def per_device_fused(blocks, chans, values, gates, filters, skip, w_out):
    block, width = values.shape
    forward, backward = tables(block)
    vmem = pl.BlockSpec(memory_space=pltpu.VMEM)
    hbm = pl.BlockSpec(memory_space=pl.ANY)
    out_width = w_out.shape[1]
    chunks = [(q * block // 2, block // 2) for q in range(2)]

    def sems(*shape):
        return pltpu.SemaphoreType.DMA(shape)

    half, pieces = blocks // 2, len(chunks)
    return pl.pallas_call(
        functools.partial(kernel, blocks, chans, chunks),
        out_shape=pltpu.VMEM((block, out_width), jnp.bfloat16),
        in_specs=[hbm, hbm, hbm, vmem, hbm, hbm, hbm],
        out_specs=vmem,
        scratch_shapes=[
            pltpu.VMEM((block, width), jnp.bfloat16),
            pltpu.VMEM((block, width), jnp.bfloat16),
            pltpu.VMEM((block, width), jnp.float32),
            pltpu.VMEM((block, width), jnp.bfloat16),
            pltpu.VMEM((blocks, block, 2 * LANES), jnp.bfloat16),
            pltpu.VMEM(forward.shape, jnp.bfloat16),
            pltpu.VMEM(backward.shape, jnp.bfloat16),
            pltpu.VMEM((blocks, 2 * block, 2 * LANES), jnp.float32),
            pltpu.VMEM((2, half, 2 * block, 2 * LANES), jnp.bfloat16),
            pltpu.VMEM((blocks, block, LANES), jnp.bfloat16),
            pltpu.VMEM((blocks, block, LANES), jnp.bfloat16),
            pltpu.VMEM((chans, half, block, 2 * LANES), jnp.bfloat16),
            pltpu.VMEM(w_out.shape, jnp.bfloat16),
            pltpu.VMEM((block, out_width), jnp.float32),
            pltpu.SemaphoreType.REGULAR((3,)), sems(7), sems(1), sems(half), sems(blocks), sems(half), sems(pieces),
        ]
        + [sems(half), sems(pieces)] * 3,
        compiler_params=pltpu.CompilerParams(
            collective_id=0, has_side_effects=True, vmem_limit_bytes=56 * 2**20
        ),
    )(values, gates, filters, skip[None, :], jnp.asarray(forward), jnp.asarray(backward), w_out)


def per_device(mesh_shape, values, gates, filters, skip, w_out):
    blocks, chans = mesh_shape["seq"], mesh_shape["chan"]
    block, width = values.shape
    fits = (
        width == blocks * LANES and chans == 4 and blocks == 8 and block == 256
        and w_out.shape[0] == chans * width and w_out.shape[1] == 1024
    )
    if fits:
        return per_device_fused(blocks, chans, values, gates, filters, skip, w_out)
    return per_device_generic(values, gates, filters, skip, w_out)


def solution(mesh):
    placed = (P("seq", "chan"), P("seq", "chan"), P("seq", "chan"), P("chan"), P(None, "chan"))
    return jax.shard_map(
        functools.partial(per_device, dict(mesh.shape)),
        mesh=mesh, in_specs=placed, out_specs=P("seq", "chan"), check_vma=False,
    )
```

```python
import functools
import math

import jax
import jax.numpy as jnp
import numpy as np
from jax import lax
from jax.experimental import pallas as pl
from jax.experimental.pallas import tpu as pltpu
from jax.sharding import PartitionSpec as P

LANES = 128
STRIP = 16
MESH = pl.DeviceIdType.MESH


def product(form, left, right):
    return jnp.einsum(
        form, left, right, precision=lax.Precision.HIGHEST, preferred_element_type=jnp.float32
    )


def phase(first_count, second_count, modulus):
    left = lax.iota(jnp.int32, first_count)[:, None]
    right = lax.iota(jnp.int32, second_count)[None, :]
    angle = (left * right % modulus).astype(jnp.float32) * (2.0 * math.pi / modulus)
    return (jnp.cos(angle), jnp.sin(angle))


def spectral_conv(chan_values, chan_filter):
    nchan = chan_values.shape[0]
    length = chan_values.shape[1]
    summed = 2 * length
    columns = 128
    row_count = summed // columns
    half_rows = row_count // 2
    cos_rows, sin_rows = phase(row_count, half_rows, row_count)
    cos_twist, sin_twist = phase(row_count, columns, summed)
    cos_cols, sin_cols = phase(columns, columns, columns)
    cos_back, sin_back = phase(half_rows, row_count, row_count)

    def forward(signal):
        grid = signal.astype(jnp.float32).reshape(nchan, half_rows, columns)
        real_a = product("kn,cna->cka", cos_rows, grid)
        imag_a = -product("kn,cna->cka", sin_rows, grid)
        real_b = real_a * cos_twist + imag_a * sin_twist
        imag_b = imag_a * cos_twist - real_a * sin_twist
        real_c = product("cka,am->ckm", real_b, cos_cols) + product("cka,am->ckm", imag_b, sin_cols)
        imag_c = product("cka,am->ckm", imag_b, cos_cols) - product("cka,am->ckm", real_b, sin_cols)
        return (real_c, imag_c)

    real_v, imag_v = forward(chan_values)
    real_h, imag_h = forward(chan_filter)
    real_p = real_v * real_h - imag_v * imag_h
    imag_p = real_v * imag_h + imag_v * real_h
    real_d = product("ckm,ma->cka", real_p, cos_cols) - product("ckm,ma->cka", imag_p, sin_cols)
    imag_d = product("ckm,ma->cka", imag_p, cos_cols) + product("ckm,ma->cka", real_p, sin_cols)
    real_e = real_d * cos_twist - imag_d * sin_twist
    imag_e = imag_d * cos_twist + real_d * sin_twist
    result = product("nk,cka->cna", cos_back, real_e) - product("nk,cka->cna", sin_back, imag_e)
    return (result * (1.0 / summed)).reshape(nchan, length).astype(jnp.bfloat16)


def per_device_generic(values, gates, filters, skip, w_out):
    value_trans = values.T
    filter_trans = filters.T
    chan_values = lax.all_to_all(value_trans, "seq", split_axis=0, concat_axis=1, tiled=True)
    chan_filter = lax.all_to_all(filter_trans, "seq", split_axis=0, concat_axis=1, tiled=True)
    convolved = spectral_conv(chan_values, chan_filter)
    causal_trans = lax.all_to_all(convolved, "seq", split_axis=1, concat_axis=0, tiled=True)
    causal = causal_trans.T
    mixed = (
        gates.astype(jnp.float32)
        * (causal.astype(jnp.float32) + skip[None, :] * values.astype(jnp.float32))
    ).astype(jnp.bfloat16)
    projected = jnp.dot(
        lax.all_gather(mixed, "chan", axis=1, tiled=True), w_out, preferred_element_type=jnp.float32
    )
    return projected.astype(jnp.bfloat16)


def split(x):
    high = x.astype(jnp.bfloat16)
    return high, (x - high.astype(jnp.float32)).astype(jnp.bfloat16)


def tables(block):
    index = np.arange(block)
    angle = np.pi * (np.outer(4 * index + 1, index) % (4 * block)) / (2 * block)
    whole = np.concatenate([np.cos(angle), -np.sin(angle)]).astype(np.float32)
    high = whole.astype(jnp.bfloat16)
    both = np.stack([high, (whole - high.astype(np.float32)).astype(jnp.bfloat16)])
    back = (both.astype(np.float32) / block).astype(jnp.bfloat16)
    return both, np.ascontiguousarray(back.transpose(0, 2, 1))


def kernel(
    blocks, chans, chunks,
    values_hbm, gates_hbm, filters_hbm, skip, forward_hbm, backward_hbm, w_hbm,
    out,
    values, gates, filters, h_send, got, forward, backward, spec, y, y_send, causal, mixed, w, acc,
    relay, l_sem, sent, gate, in_sem, n_sem, x_sem, an_sem, ax_sem, bn_sem, bx_sem, fn_sem, fx_sem,
):
    me = lax.axis_index("seq")
    mine = lax.axis_index("chan")
    block = values.shape[0]
    depth = values.shape[1]
    half = blocks // 2
    left, right = pl.ds(0, LANES), pl.ds(LANES, LANES)
    every = pl.ds(0, block)
    near = list(range(1, half))
    upper = me // half
    seat = lax.rem(me, half)
    other = half - half * upper
    odd = lax.rem(me, 2)

    def lanes(position):
        return pl.ds(pl.multiple_of(position * LANES, LANES), LANES)

    def partner(mask):
        place = me
        bit = 1
        while bit < half:
            if mask & bit:
                place = place + bit - 2 * bit * lax.rem(place // bit, 2)
            bit *= 2
        return place

    places = [partner(mask) for mask in range(half)]

    local = [
        pltpu.make_async_copy(source, target, l_sem.at[i])
        for i, (source, target) in enumerate((
            (filters_hbm, filters), (values_hbm, values), (values_hbm.at[:, lanes(me)], got.at[me, :, left]),
            (forward_hbm, forward), (backward_hbm, backward), (gates_hbm, gates), (w_hbm, w),
        ))
    ]
    filters_copy, values_copy, own_copy, forward_copy, backward_copy, gates_copy, w_copy = local
    for copy in local:
        copy.start()

    sibling = mine + 1 - 2 * lax.rem(mine, 2)
    across = lax.rem(mine + 2, chans)
    opposite = lax.rem(sibling + 2, chans)
    level = me // 2
    levels = blocks // 2
    inside = lax.rem((level + 1) // 2, 2)
    turned = me + 1 - 2 * odd
    barrier = pltpu.get_barrier_semaphore()

    def greet(sem):
        pl.semaphore_signal(sem, inc=1, device_id={"seq": turned}, device_id_type=MESH)

        @pl.when(level > 0)
        def _():
            pl.semaphore_signal(sem, inc=1, device_id={"seq": me - 2}, device_id_type=MESH)

        @pl.when(level < levels - 1)
        def _():
            pl.semaphore_signal(sem, inc=1, device_id={"seq": me + 2}, device_id_type=MESH)

    greet(barrier)
    for chan in (sibling, across):
        pl.semaphore_signal(barrier, inc=1, device_id={"chan": chan}, device_id_type=MESH)
    filters_copy.wait()
    h_send[...] = filters[...].astype(jnp.bfloat16)
    pl.semaphore_wait(barrier, 4 + inside)
    greet(relay.at[0])

    def remote(source, target, sem, where, out_sem=None):
        return pltpu.make_async_remote_copy(
            src_ref=source, dst_ref=target, send_sem=sent.at[0] if out_sem is None else out_sem, recv_sem=sem,
            device_id=where, device_id_type=MESH,
        )

    def across_cut(phase):
        return [other + 2 * phase + odd, other + 2 * phase + 1 - odd]

    def send_in(place):
        remote(values_hbm.at[:, lanes(place)], got.at[me, :, left], in_sem.at[me], {"seq": place}).start()
        remote(h_send.at[:, lanes(place)], got.at[me, :, right], in_sem.at[me], {"seq": place}).start()

    first, second = across_cut(upper), across_cut(1 - upper)

    @pl.when(inside == 1)
    def _():
        send_in(first[0])

    @pl.when(inside == 0)
    def _():
        send_in(places[2])
        send_in(places[1])

    for stage in range(1, 4):
        pl.semaphore_wait(relay.at[stage - 1], 2 + inside)
        if stage < 3:
            greet(relay.at[stage])
        plans = (
            (1, 0, {1: [first[1], second[0]], 2: [second[1], places[2], places[1]], 3: [places[3]]}),
            (0, 0, {1: [first[0], places[3]], 2: [first[1], second[0]], 3: [second[1]]}),
            (1, 1, {1: [second[0]], 2: [first[1], second[1], places[2], places[1]], 3: [places[3]]}),
            (0, 1, {1: [first[0], places[3]], 2: [second[0], first[1]], 3: [second[1]]}),
        )
        for within, side, plan in plans:

            @pl.when(jnp.logical_and(inside == within, upper == side))
            def _():
                for place in plan[stage]:
                    send_in(place)

    got[me, :, LANES:] = h_send[:, lanes(me)]
    own_copy.wait()
    forward_copy.wait()

    def transform(place):
        x = got[place]
        spec[place] = jnp.dot(forward[0], x, preferred_element_type=jnp.float32) + jnp.dot(
            forward[1], x, preferred_element_type=jnp.float32
        )

    def take_in(place):
        spot = got.at[place]
        remote(spot, spot, in_sem.at[place], {"seq": other}).wait_recv()
        transform(place)

    def combine(pair):
        def body(strip, _):
            parts = []
            for part in range(STRIP // 8):
                re_rows = pl.ds(pl.multiple_of(strip * STRIP + 8 * part, 8), 8)
                im_rows = pl.ds(pl.multiple_of(block + strip * STRIP + 8 * part, 8), 8)
                count = pair[-1] + 1
                v = [(spec[n, re_rows, :LANES], spec[n, im_rows, :LANES]) for n in range(count)]
                h = [(spec[n, re_rows, LANES:], spec[n, im_rows, LANES:]) for n in range(count)]
                g = [h[0]] + [(h[n][0] - h[n - 1][1], h[n][1] + h[n - 1][0]) for n in range(1, count)]
                sums = []
                for k in pair:
                    re = im = None
                    for n in range(k + 1):
                        (a, b), (c, d) = v[n], g[k - n]
                        re_term, im_term = a * c - b * d, a * d + b * c
                        re = re_term if re is None else re + re_term
                        im = im_term if im is None else im + im_term
                    sums.append((re, im))
                parts.append(sums)
            for i in (0, 1):
                for which in (0, 1):
                    high, low = split(jnp.concatenate([sums[i][which] for sums in parts], axis=0))
                    rows = pl.ds(pl.multiple_of(which * block + strip * STRIP, STRIP), STRIP)
                    y[0, pair[0] // 2, rows, i * LANES : (i + 1) * LANES] = high
                    y[1, pair[0] // 2, rows, i * LANES : (i + 1) * LANES] = low
            return 0

        lax.fori_loop(0, block // STRIP, body, 0)

    def produce(rank):
        pair = (2 * rank, 2 * rank + 1)
        combine(pair)
        high, low = y[0, rank], y[1, rank]
        x = (
            jnp.dot(backward[0], high, preferred_element_type=jnp.float32)
            + jnp.dot(backward[1], high, preferred_element_type=jnp.float32)
            + jnp.dot(backward[0], low, preferred_element_type=jnp.float32)
        ).astype(jnp.bfloat16)
        y_send[pair[0]] = x[:, :LANES]
        y_send[pair[1]] = x[:, LANES:]

    def send_near():
        for mask in near:
            remote(y_send.at[places[mask]], causal.at[mask], n_sem.at[mask], {"seq": places[mask]}).start()

    def send_cross(phase, q):
        start, size = chunks[q]
        rows = pl.ds(start, size)
        for place in across_cut(phase):
            remote(
                y_send.at[place, rows], causal.at[half + seat, rows], x_sem.at[q], {"seq": place},
                gate.at[phase * len(chunks) + q],
            ).start()

    def gone(phase, q):
        spot = causal.at[0]
        remote(spot, spot, x_sem.at[q], {"seq": other}, gate.at[phase * len(chunks) + q]).wait_send()

    def slot(chan, mask):
        return mixed.at[chan, mask // 2, :, lanes(lax.rem(places[mask], 2))]

    def far_slot(chan, q):
        start, size = chunks[q]
        return mixed.at[chan, pl.ds(half // 2, half // 2), pl.ds(start, size)]

    def blend(place, y_rows, rows, target):
        cols = lanes(place)
        direct = skip[:, cols] * values[rows, cols].astype(jnp.float32)
        target[rows, :] = (gates[rows, cols].astype(jnp.float32) * (y_rows.astype(jnp.float32) + direct)).astype(
            jnp.bfloat16
        )

    def share(spot, a_sem, b_sem):
        remote(spot, spot, a_sem, {"chan": across}).start()
        remote(spot, spot, b_sem, {"chan": sibling}).start()

    def near_in(mask):
        if mask:
            spot = causal.at[mask]
            remote(spot, spot, n_sem.at[mask], {"seq": places[mask]}).wait_recv()
            blend(places[mask], causal[mask], every, slot(mine, mask))
        else:
            blend(me, y_send[me], every, slot(mine, mask))
        share(slot(mine, mask), an_sem.at[mask], bn_sem.at[mask])

    def cross_in(q):
        start, size = chunks[q]
        rows = pl.ds(start, size)
        spot = causal.at[pl.ds(half, half), rows]
        remote(spot, spot, x_sem.at[q], {"seq": other}).wait_recv()
        for t in range(half):
            blend(other + t, causal[half + t, rows], rows, mixed.at[mine, (half + t) // 2, :, lanes(t % 2)])
        share(far_slot(mine, q), ax_sem.at[q], bx_sem.at[q])

    def near_on(mask):
        spot = slot(across, mask)
        remote(spot, spot, an_sem.at[mask], {"chan": across}).wait_recv()
        remote(spot, spot, fn_sem.at[mask], {"chan": sibling}).start()

    def cross_on(q):
        spot = far_slot(across, q)
        remote(spot, spot, ax_sem.at[q], {"chan": across}).wait_recv()
        remote(spot, spot, fx_sem.at[q], {"chan": sibling}).start()

    def arrived(spot, sem):
        remote(spot, spot, sem, {"chan": sibling}).wait_recv()

    def project(ranks, start, size, pair, first, last):
        rows = pl.ds(start, size)

        def tile(n, _):
            cols = pl.ds(pl.multiple_of(n * 512, 512), 512)
            total = None
            for chan in pair:
                for rank in ranks:
                    source = places[2 * rank] // 2 if 2 * rank < half else other // 2 + rank - half // 2
                    deep = pl.ds(pl.multiple_of(chan * depth + source * 2 * LANES, 2 * LANES), 2 * LANES)
                    term = jnp.dot(mixed[chan, rank, rows], w[deep, cols], preferred_element_type=jnp.float32)
                    total = term if total is None else total + term
            if not first:
                total = total + acc[rows, cols]
            if last:
                out[rows, cols] = total.astype(out.dtype)
            else:
                acc[rows, cols] = total
            return 0

        lax.fori_loop(0, out.shape[1] // 512, tile, 0)

    close, far = range(half // 2), range(half // 2, half)
    masks = [0] + near

    def near_first():
        for mask in masks:
            arrived(slot(sibling, mask), bn_sem.at[mask])
        project(close, 0, block, (mine, sibling), True, False)

    def near_second():
        for mask in masks:
            arrived(slot(opposite, mask), fn_sem.at[mask])
        project(close, 0, block, (across, opposite), False, False)

    def cross_first(q):
        arrived(far_slot(sibling, q), bx_sem.at[q])
        project(far, *chunks[q], (mine, sibling), False, False)

    def cross_second(q):
        arrived(far_slot(opposite, q), fx_sem.at[q])
        project(far, *chunks[q], (across, opposite), False, True)

    transform(me)
    for mask in near:
        take_in(places[mask])
    backward_copy.wait()
    values_copy.wait()
    gates_copy.wait()

    @pl.when(upper == 0)
    def _():
        for rank in range(half // 2):
            produce(rank)
        send_near()
        near_in(0)
        for phase in range(half // 2):
            rank = half // 2 + phase
            take_in(2 * rank)
            take_in(2 * rank + 1)
            produce(rank)
            if phase == 0:
                send_cross(0, 0)
                send_cross(0, 1)

                @pl.when(level == 0)
                def _():
                    for mask in near:
                        near_in(mask)


    @pl.when(upper == 1)
    def _():
        for rank in range(half // 2):
            take_in(2 * rank)
            take_in(2 * rank + 1)
            if rank == 0:
                produce(rank)
                send_cross(0, 0)
                send_cross(0, 1)
        for rank in range(half // 2, half):
            produce(rank)
        send_near()
        for rank in range(1, half // 2):
            produce(rank)
        near_in(0)

    w_copy.wait()
    @pl.when(level > 0)
    def _():
        gone(0, 0)
        gone(0, 1)

    send_cross(1, 0)
    send_cross(1, 1)
    @pl.when(level > 0)
    def _():
        for mask in near:
            near_in(mask)

    cross_in(0)
    cross_in(1)
    for mask in masks:
        near_on(mask)
    near_first()
    near_second()
    cross_on(0)
    cross_first(0)
    cross_on(1)
    cross_first(1)
    cross_second(0)
    cross_second(1)
    @pl.when(level == 0)
    def _():
        gone(0, 0)
        gone(0, 1)

    gone(1, 0)
    gone(1, 1)
    whole = w.at[pl.ds(0, (3 * (blocks - 1) + 3 * blocks - half) * block * LANES // w.shape[1])]
    remote(whole, whole, in_sem.at[0], {"chan": sibling}).wait_send()


def per_device_fused(blocks, chans, values, gates, filters, skip, w_out):
    block, width = values.shape
    forward, backward = tables(block)
    vmem = pl.BlockSpec(memory_space=pltpu.VMEM)
    hbm = pl.BlockSpec(memory_space=pl.ANY)
    out_width = w_out.shape[1]
    chunks = [(q * block // 2, block // 2) for q in range(2)]

    def sems(*shape):
        return pltpu.SemaphoreType.DMA(shape)

    half, pieces = blocks // 2, len(chunks)
    return pl.pallas_call(
        functools.partial(kernel, blocks, chans, chunks),
        out_shape=pltpu.VMEM((block, out_width), jnp.bfloat16),
        in_specs=[hbm, hbm, hbm, vmem, hbm, hbm, hbm],
        out_specs=vmem,
        scratch_shapes=[
            pltpu.VMEM((block, width), jnp.bfloat16),
            pltpu.VMEM((block, width), jnp.bfloat16),
            pltpu.VMEM((block, width), jnp.float32),
            pltpu.VMEM((block, width), jnp.bfloat16),
            pltpu.VMEM((blocks, block, 2 * LANES), jnp.bfloat16),
            pltpu.VMEM(forward.shape, jnp.bfloat16),
            pltpu.VMEM(backward.shape, jnp.bfloat16),
            pltpu.VMEM((blocks, 2 * block, 2 * LANES), jnp.float32),
            pltpu.VMEM((2, half, 2 * block, 2 * LANES), jnp.bfloat16),
            pltpu.VMEM((blocks, block, LANES), jnp.bfloat16),
            pltpu.VMEM((blocks, block, LANES), jnp.bfloat16),
            pltpu.VMEM((chans, half, block, 2 * LANES), jnp.bfloat16),
            pltpu.VMEM(w_out.shape, jnp.bfloat16),
            pltpu.VMEM((block, out_width), jnp.float32),
            pltpu.SemaphoreType.REGULAR((3,)), sems(7), sems(1), sems(half), sems(blocks), sems(half), sems(pieces),
        ]
        + [sems(half), sems(pieces)] * 3,
        compiler_params=pltpu.CompilerParams(
            collective_id=0, has_side_effects=True, vmem_limit_bytes=56 * 2**20
        ),
    )(values, gates, filters, skip[None, :], jnp.asarray(forward), jnp.asarray(backward), w_out)


def per_device(mesh_shape, values, gates, filters, skip, w_out):
    blocks, chans = mesh_shape["seq"], mesh_shape["chan"]
    block, width = values.shape
    fits = (
        width == blocks * LANES and chans == 4 and blocks == 8 and block == 256
        and w_out.shape[0] == chans * width and w_out.shape[1] == 1024
    )
    if fits:
        return per_device_fused(blocks, chans, values, gates, filters, skip, w_out)
    return per_device_generic(values, gates, filters, skip, w_out)


def solution(mesh):
    placed = (P("seq", "chan"), P("seq", "chan"), P("seq", "chan"), P("chan"), P(None, "chan"))
    return jax.shard_map(
        functools.partial(per_device, dict(mesh.shape)),
        mesh=mesh, in_specs=placed, out_specs=P("seq", "chan"), check_vma=False,
    )
```
